128 devices in a mesh: ha: 8 (over z, core), wa: 16 (over y, x).
Axes of the slice: x: 4, y: 4, z: 4, core: 2. Of those that a mesh axis runs over, the one named last changes fastest.
Arguments:
- features: bfloat16 [256, 512, 256], P('ha', 'wa'), may hold values from -6 to 6
- counts: int32 [8, 16], P('ha', 'wa'), may hold values from 0 to 16, as said below
- owner_perm: int32 [8, 16], P('ha'), may hold values from 0 to 15, each once within a row
- corners: int32 [2048, 2], P(('ha', 'wa')), may hold values from 0 to 31, as said below
- offsets: int32 [2048, 28], P(('ha', 'wa')), may hold values from 0 to 124
- kernels: bfloat16 [2, 3, 3, 256, 256], replicated, may hold values from -0.125 to 0.125
- cotangent: bfloat16 [1024, 14, 14, 256], P(('ha', 'wa')), may hold values from -6 to 6
Outputs:
- grad_features: float32 [256, 512, 256], P('ha', 'wa')
- grad_kernels: float32 [2, 3, 3, 256, 256], replicated
The draws below stay inside these ranges and needn't reach their ends.
Inputs may be any that keep to these rules, and one draw needn't show every extreme that they name: In each row of tiles the counts add up to 8 times the number of devices along wa, and one tile of every row has exactly 16. `corners`: the first column is below 32, the second below 32.
All inputs are finite; a program needn't handle non-finite values.
Results may differ from the reference program's by a relative error of at most 0.012.
Values may be sent and summed in bfloat16 or wider, within the bound.
No kernel may reach another device: no remote copies, remote signals or barrier semaphores. Data moves between devices by JAX's collectives and lax.ppermute only.
A program may use at most 192 MiB of HBM per device.

```python
import jax
import jax.numpy as jnp
from jax import lax

TH = 32
TW = 32
C = 256
SIDE = 14
BOX = 32
LAYERS = 2
REG_DEV = 8
TILE_REGION_MAX = 16
H = 256
W = 512
REG = 1024
SLOTS = 2048
N_HA = 8
N_WA = 16


def draw_counts(key, part):

    def one_row(random_row_key):
        selection_key, extra_priority_key, ranking_key = jax.random.split(random_row_key, 3)
        chosen = jax.random.randint(selection_key, (), 0, N_WA)
        extra_priority = jax.random.randint(extra_priority_key, (N_WA,), 0, 2)
        region_ranking = jax.random.permutation(ranking_key, N_WA * TILE_REGION_MAX).astype(jnp.int32)
        owning_tile = jnp.arange(N_WA * TILE_REGION_MAX, dtype=jnp.int32) // TILE_REGION_MAX
        region_score = extra_priority[owning_tile] * (N_WA * TILE_REGION_MAX) + region_ranking
        region_score = jnp.where(owning_tile == chosen, -1 - region_ranking, region_score)
        ignored, picked = lax.top_k(region_score, REG_DEV * N_WA - TILE_REGION_MAX)
        taken = jnp.sum((owning_tile[picked][:, None] == jnp.arange(N_WA, dtype=jnp.int32)[None, :]).astype(jnp.int32), axis=0)
        return (taken + TILE_REGION_MAX * (jnp.arange(N_WA, dtype=jnp.int32) == chosen).astype(jnp.int32)).astype(jnp.int32)
    row_keys = jax.random.split(jax.random.fold_in(key, 7), N_HA)
    return jax.vmap(one_row)(row_keys)


def draw_corners(key, part):
    random_row_key, col_key = jax.random.split(jax.random.fold_in(key, 11))
    top_rows = jax.random.randint(random_row_key, (N_HA * N_WA * TILE_REGION_MAX, 1), 0, TH)
    left_cols = jax.random.randint(col_key, (N_HA * N_WA * TILE_REGION_MAX, 1), 0, TW)
    return jnp.concatenate([top_rows, left_cols], axis=1).astype(jnp.int32)


def plant(values, key, low, largest):
    longest = values.shape.index(max(values.shape))
    spots = []
    for shift in (0, 1):
        where = [jax.random.randint(jax.random.fold_in(key, axis), (), 0, length) for axis, length in enumerate(values.shape)]
        where[longest] = (where[longest] + shift) % values.shape[longest]
        spots.append(tuple(where))
    return values.at[spots[0]].set(low).at[spots[1]].set(largest)


def steps_of(own_key, shape, pieces, least, top_value):
    level = 1.0
    for position, shards_of in pieces:
        steps = jax.random.uniform(jax.random.fold_in(jax.random.fold_in(own_key, 6), position), (shards_of,), jnp.float32, least / len(pieces), top_value / len(pieces))
        level = level * jnp.repeat(jnp.exp(steps), shape[position] // shards_of).reshape((-1,) + (1,) * (len(shape) - 1 - position))
    return level


def normal_values(own_key, extent, scale, bound, cuts=(), kind=jnp.bfloat16):
    values = scale * jax.random.normal(own_key, extent, jnp.float32)
    if cuts:
        values = values * steps_of(own_key, extent, cuts, -0.22, 0.18)
    return jnp.clip(values, -bound, bound).astype(kind)


def setup_inputs(seed: int = 0) -> dict:
    key_list = jax.random.split(jax.random.key(seed), 8)
    features = normal_values(key_list[0], (H, W, C), 1.0, 6.0, ((0, 8), (1, 16)))
    counts = draw_counts(jax.random.fold_in(key_list[7], 71), 0)
    owner_perm = jax.vmap(lambda own: jax.random.permutation(own, N_WA))(jax.random.split(key_list[2], N_HA)).reshape((N_HA, N_WA)).astype(jnp.int32)
    corners = draw_corners(jax.random.fold_in(key_list[7], 71), 0)
    offsets = plant(jax.random.randint(key_list[4], (SLOTS, 2 * SIDE), 0, 4 * BOX - 3), jax.random.fold_in(key_list[4], 1), 0, (4 * BOX - 3) - 1).astype(jnp.int32)
    kernels = normal_values(key_list[5], (LAYERS, 3, 3, C, C), (9 * C) ** -0.5, 0.125)
    cotangent = normal_values(key_list[6], (REG, SIDE, SIDE, C), 1.0, 6.0, ((0, 128),))
    return dict(features=features, counts=counts, owner_perm=owner_perm, corners=corners, offsets=offsets, kernels=kernels, cotangent=cotangent)


highest = lax.Precision.HIGHEST

def tent_weights(sample_offsets):
    places = 4 * jnp.arange(BOX, dtype=jnp.int32)
    spread = jnp.abs(places[None, :] - sample_offsets[..., :, None]).astype(jnp.float32)
    return jnp.maximum(0.0, 1.0 - spread / 4.0)

def convolve(inputs, kernel):
    return lax.conv_general_dilated(inputs, kernel, (1, 1), 'SAME', dimension_numbers=('NHWC', 'HWIO', 'NHWC'), precision=highest)

def gelu_exact(values):
    return jax.nn.gelu(values, approximate=False)

def reference(features, counts, owner_perm, corners, offsets, kernels, cotangent):
    row_tiles, col_tiles = counts.shape
    slot_total = corners.shape[0]
    capacity = slot_total // (row_tiles * col_tiles)
    regions = cotangent.shape[0]
    channels = features.shape[2]
    height, breadth = (features.shape[0], features.shape[1])
    slot_ids = jnp.arange(slot_total, dtype=jnp.int32)
    tile_ids = slot_ids // capacity
    within = slot_ids % capacity
    tile_row = tile_ids // col_tiles
    tile_col = tile_ids % col_tiles
    starts = (jnp.cumsum(counts, axis=1) - counts).astype(jnp.int32)
    live_slot = within < counts[tile_row, tile_col]
    stream = (starts[tile_row, tile_col] + within).astype(jnp.int32)
    owner_slot = (tile_row * col_tiles + owner_perm[tile_row, stream % col_tiles]) * REG_DEV + stream // col_tiles
    target = jnp.where(live_slot, owner_slot, regions).astype(jnp.int32)
    source = jnp.zeros((regions,), jnp.int32).at[target].set(slot_ids, mode='drop')
    top_rows = (tile_row * TH + corners[:, 0]).astype(jnp.int32)
    left_cols = (tile_col * TW + corners[:, 1]).astype(jnp.int32)
    padded = jnp.pad(features, ((0, BOX), (0, BOX), (0, 0)))

    def block_step(running, region_ids):
        grad_map, kernel_sum = running
        chosen = source[region_ids]
        block_tops = top_rows[chosen]
        block_lefts = left_cols[chosen]
        windows = jax.vmap(lambda top_row, left_col: lax.dynamic_slice(padded, (top_row, left_col, jnp.int32(0)), (BOX, BOX, channels)))(block_tops, block_lefts)
        row_weights = tent_weights(offsets[chosen, :SIDE])
        col_weights = tent_weights(offsets[chosen, SIDE:])
        partial_rows = jnp.einsum('nip,npqc->niqc', row_weights, windows.astype(jnp.float32), precision=highest)
        samples = jnp.einsum('njq,niqc->nijc', col_weights, partial_rows, precision=highest).astype(jnp.bfloat16)
        inputs = [samples]
        before = []
        for layer_step in range(LAYERS):
            values = convolve(inputs[layer_step].astype(jnp.float32), kernels[layer_step].astype(jnp.float32))
            before.append(values)
            inputs.append(gelu_exact(values).astype(jnp.bfloat16))
        upward = cotangent[region_ids]
        layer_grads = [None] * LAYERS
        for layer_step in reversed(range(LAYERS)):
            ignored, gelu_slope = jax.vjp(gelu_exact, before[layer_step])
            inner_grad = gelu_slope(upward.astype(jnp.float32))[0].astype(jnp.bfloat16)
            ignored, pullback = jax.vjp(convolve, inputs[layer_step].astype(jnp.float32), kernels[layer_step].astype(jnp.float32))
            input_grad, kernel_grad = pullback(inner_grad.astype(jnp.float32))
            layer_grads[layer_step] = kernel_grad
            upward = input_grad.astype(jnp.bfloat16)
        spread_cols = jnp.einsum('njq,nijc->niqc', col_weights, upward.astype(jnp.float32), precision=highest)
        window_grads = jnp.einsum('nip,niqc->npqc', row_weights, spread_cols, precision=highest)
        for member in range(region_ids.shape[0]):
            corner_at = (block_tops[member], block_lefts[member], jnp.int32(0))
            current = lax.dynamic_slice(grad_map, corner_at, (BOX, BOX, channels))
            grad_map = lax.dynamic_update_slice(grad_map, current + window_grads[member], corner_at)
        return ((grad_map, kernel_sum + jnp.stack(layer_grads)), None)
    blocks = jnp.arange(regions, dtype=jnp.int32).reshape(regions // 8, 8)
    start_map = jnp.zeros((height + BOX, breadth + BOX, channels), jnp.float32)
    start_sum = jnp.zeros((LAYERS, 3, 3, channels, channels), jnp.float32)
    (grad_map, kernel_sum), ignored = lax.scan(block_step, (start_map, start_sum), blocks)
    return (grad_map[:height, :breadth], kernel_sum)
```

```python
import functools

import jax
import jax.numpy as jnp
from jax import lax
from jax.experimental import pallas as pl
from jax.experimental.pallas import tpu as pltpu
from jax.sharding import PartitionSpec as P

SIDE = 14
PITCH = 16
PIX = SIDE * PITCH
BOX = 32
SPAN = 48
WIN = BOX * SPAN
ROWS = 288
C = 256
BF = jnp.bfloat16
F32 = jnp.float32


def shifted(value, axis, steps):
    count = lax.axis_size(axis)
    first, last = (max(0, -steps), min(count, count - steps))
    return lax.ppermute(value, axis, [(source, source + steps) for source in range(first, last)])


def dot(a, b, dims=(((1,), (0,)), ((), ()))):
    return lax.dot_general(a, b, dims, preferred_element_type=F32)


def inside(rows):
    pixel = lax.broadcasted_iota(jnp.int32, (rows, C), 0)
    return (pixel & (PITCH - 1)) < SIDE


def clear_edges(held, copies):
    for shift in range(3):
        for g in range(copies):
            held[shift, g, 0:16, :] = jnp.zeros((16, C), BF)
            held[shift, g, 16 + PIX : ROWS, :] = jnp.zeros((ROWS - 16 - PIX, C), BF)


def hold(held, g, value):
    held[0, g, 16 : 16 + PIX, :] = pltpu.roll(value, 1, 0).astype(BF)
    held[1, g, 16 : 16 + PIX, :] = value.astype(BF)
    held[2, g, 16 : 16 + PIX, :] = pltpu.roll(value, PIX - 1, 0).astype(BF)


def tent(places, offsets):
    return jnp.maximum(0.0, 1.0 - jnp.abs(places - offsets) * 0.25)


def gelu_parts(v):
    cdf = 0.5 * (1.0 + lax.erf(v * 0.7071067811865476))
    slope = cdf + v * (jnp.exp(v * v * -0.5) * 0.3989422804014327)
    return v * cdf, slope


def route_kernel(index_ref, x_ref, o_ref):
    o_ref[0, :, 0:SIDE, :] = x_ref[0]
    o_ref[0, :, SIDE:PITCH, :] = jnp.zeros((SIDE, PITCH - SIDE, C), BF)


def route(index, cotangent):
    peers = index.shape[0]
    return pl.pallas_call(
        route_kernel,
        name="route",
        out_shape=jax.ShapeDtypeStruct((peers, SIDE, PITCH, C), BF),
        grid_spec=pltpu.PrefetchScalarGridSpec(
            num_scalar_prefetch=1,
            grid=(peers,),
            in_specs=[pl.BlockSpec((1, SIDE, SIDE, C), lambda i, index: (index[i], 0, 0, 0))],
            out_specs=pl.BlockSpec((1, SIDE, PITCH, C), lambda i, index: (i, 0, 0, 0)),
        ),
        cost_estimate=pl.CostEstimate(flops=0, bytes_accessed=4 << 20, transcendentals=0),
    )(index, cotangent)


FG = 2


def forward_kernel(
    corner_ref, tl_ref, tr_ref, bl_ref, br_ref, off_ref, place_ref, k_ref,
    a0_ref, a1_ref, g0_ref, g1_ref, ext, row_w, weight, held,
):
    step = pl.program_id(0)

    @pl.when(step == 0)
    def _():
        clear_edges(held, FG)
        ext[0:BOX, 0:BOX, :] = tl_ref[...]
        ext[0:BOX, BOX : 2 * BOX, :] = tr_ref[...]
        ext[BOX : 2 * BOX, 0:BOX, :] = bl_ref[...]
        ext[BOX : 2 * BOX, BOX : 2 * BOX, :] = br_ref[...]

    keep = inside(PIX)
    for g in range(FG):
        slot = step * FG + g
        top = corner_ref[slot, 0]
        left = pl.multiple_of(corner_ref[slot, 1] // 16 * 16, 16)
        rows = off_ref[g, 0:16, 0:1]
        cols = off_ref[g, 16:32, 0:1]
        row_w[g] = tent(place_ref[0:1, :], rows)
        col_w = tent(place_ref[1:2, :], cols)
        for i in range(SIDE):
            weight[g, i * PITCH : (i + 1) * PITCH, :] = (row_w[g, i : i + 1, :] * col_w).astype(BF)
        window = ext[pl.ds(top, BOX), pl.ds(left, SPAN), :].reshape(WIN, C)
        hold(held, g, dot(weight[g], window))
        a0_ref[:, g * C : (g + 1) * C] = held[1, g, 16 : 16 + C, :].T
    for layer in range(2):
        for g in range(FG):
            pre = jnp.zeros((PIX, C), F32)
            for dy in range(3):
                for dx in range(3):
                    pre += dot(held[dx, g, 16 * dy : 16 * dy + PIX, :], k_ref[layer, dy * 3 + dx])
            value, slope = gelu_parts(pre)
            slope = jnp.where(keep, slope, 0.0).astype(BF)
            if layer == 0:
                g0_ref[g] = slope
                hold(held, g, jnp.where(keep, value, 0.0))
                a1_ref[:, g * C : (g + 1) * C] = held[1, g, 16 : 16 + C, :].T
            else:
                g1_ref[g] = slope


def forward(corners, pieces, off_cols, places, kernels):
    slots = corners.shape[0]
    whole = lambda *shape: pl.BlockSpec(shape, lambda i, *_: (0,) * len(shape))
    return pl.pallas_call(
        forward_kernel,
        name="forward",
        out_shape=[
            jax.ShapeDtypeStruct((C, slots * C), BF),
            jax.ShapeDtypeStruct((C, slots * C), BF),
            jax.ShapeDtypeStruct((slots, PIX, C), BF),
            jax.ShapeDtypeStruct((slots, PIX, C), BF),
        ],
        grid_spec=pltpu.PrefetchScalarGridSpec(
            num_scalar_prefetch=1,
            grid=(slots // FG,),
            in_specs=[whole(BOX, BOX, C)] * 4
            + [
                pl.BlockSpec((FG, 32, 128), lambda i, *_: (i, 0, 0)),
                whole(8, WIN),
                whole(2, 9, C, C),
            ],
            out_specs=[
                pl.BlockSpec((C, FG * C), lambda i, *_: (0, i)),
                pl.BlockSpec((C, FG * C), lambda i, *_: (0, i)),
                pl.BlockSpec((FG, PIX, C), lambda i, *_: (i, 0, 0)),
                pl.BlockSpec((FG, PIX, C), lambda i, *_: (i, 0, 0)),
            ],
            scratch_shapes=[
                pltpu.VMEM((2 * BOX, 2 * BOX, C), BF),
                pltpu.VMEM((FG, 16, WIN), F32),
                pltpu.VMEM((FG, PIX, WIN), BF),
                pltpu.VMEM((3, FG, ROWS, C), BF),
            ],
        ),
        cost_estimate=pl.CostEstimate(
            flops=11_300_000_000, bytes_accessed=12 << 20, transcendentals=4_000_000
        ),
    )(corners, *pieces, off_cols, places, kernels)


BG = 4


def top_grad(meta_ref, slot, in_ref, g1_ref, g):
    source = meta_ref[slot]
    live = slot < meta_ref[16]
    grad = in_ref[source].astype(F32) * g1_ref[g].astype(F32)
    return jnp.where(live, grad, 0.0)


def kernel_grad(step, steps, held, a_ref, acc, o_ref):
    @pl.when(step == 0)
    def _():
        acc[...] = jnp.zeros_like(acc)

    for dy in range(3):
        for dx in range(3):
            grads = held[2 - dx, :, 32 - 16 * dy : 32 - 16 * dy + C, :].reshape(BG * C, C)
            acc[dy * 3 + dx] += dot(a_ref[...], grads)

    @pl.when(step == steps - 1)
    def _():
        o_ref[...] = acc[...].astype(BF)


def last_kernel(meta_ref, in_ref, g1_ref, a_ref, o_ref, held, acc):
    step = pl.program_id(0)

    @pl.when(step == 0)
    def _():
        clear_edges(held, BG)

    for g in range(BG):
        hold(held, g, top_grad(meta_ref, step * BG + g, in_ref, g1_ref, g))
    kernel_grad(step, pl.num_programs(0), held, a_ref, acc, o_ref)


def last_grad(meta, incoming, slope1, acts1):
    slots = slope1.shape[0]
    return pl.pallas_call(
        last_kernel,
        name="last_grad",
        out_shape=jax.ShapeDtypeStruct((9, C, C), BF),
        grid_spec=pltpu.PrefetchScalarGridSpec(
            num_scalar_prefetch=1,
            grid=(slots // BG,),
            in_specs=[
                pl.BlockSpec((16, PIX, C), lambda i, *_: (0, 0, 0)),
                pl.BlockSpec((BG, PIX, C), lambda i, *_: (i, 0, 0)),
                pl.BlockSpec((C, BG * C), lambda i, *_: (0, i)),
            ],
            out_specs=pl.BlockSpec((9, C, C), lambda i, *_: (0, 0, 0)),
            scratch_shapes=[pltpu.VMEM((3, BG, ROWS, C), BF), pltpu.VMEM((9, C, C), F32)],
        ),
        cost_estimate=pl.CostEstimate(
            flops=4_800_000_000, bytes_accessed=8 << 20, transcendentals=0
        ),
    )(meta, incoming, slope1, acts1)


def input_grad(held, g, k_ref):
    total = jnp.zeros((PIX, C), F32)
    for dy in range(3):
        for dx in range(3):
            total += dot(
                held[2 - dx, g, 32 - 16 * dy : 32 - 16 * dy + PIX, :],
                k_ref[dy * 3 + dx],
                (((1,), (1,)), ((), ())),
            )
    return total.astype(BF)


def middle_kernel(
    meta_ref, in_ref, g1_ref, g0_ref, k_ref, a_ref, p_ref, o_ref, upper, held, acc
):
    step = pl.program_id(0)

    @pl.when(step == 0)
    def _():
        clear_edges(upper, BG)
        clear_edges(held, BG)

    for g in range(BG):
        hold(upper, g, top_grad(meta_ref, step * BG + g, in_ref, g1_ref, g))
    for g in range(BG):
        grad = input_grad(upper, g, k_ref).astype(F32) * g0_ref[g].astype(F32)
        p_ref[g] = grad.astype(BF)
        hold(held, g, grad)
    kernel_grad(step, pl.num_programs(0), held, a_ref, acc, o_ref)


def middle_grad(meta, incoming, slope1, slope0, kernel1, acts0):
    slots = slope1.shape[0]
    return pl.pallas_call(
        middle_kernel,
        name="middle_grad",
        out_shape=[
            jax.ShapeDtypeStruct((slots, PIX, C), BF),
            jax.ShapeDtypeStruct((9, C, C), BF),
        ],
        grid_spec=pltpu.PrefetchScalarGridSpec(
            num_scalar_prefetch=1,
            grid=(slots // BG,),
            in_specs=[
                pl.BlockSpec((16, PIX, C), lambda i, *_: (0, 0, 0)),
                pl.BlockSpec((BG, PIX, C), lambda i, *_: (i, 0, 0)),
                pl.BlockSpec((BG, PIX, C), lambda i, *_: (i, 0, 0)),
                pl.BlockSpec((9, C, C), lambda i, *_: (0, 0, 0)),
                pl.BlockSpec((C, BG * C), lambda i, *_: (0, i)),
            ],
            out_specs=[
                pl.BlockSpec((BG, PIX, C), lambda i, *_: (i, 0, 0)),
                pl.BlockSpec((9, C, C), lambda i, *_: (0, 0, 0)),
            ],
            scratch_shapes=[
                pltpu.VMEM((3, BG, ROWS, C), BF),
                pltpu.VMEM((3, BG, ROWS, C), BF),
                pltpu.VMEM((9, C, C), F32),
            ],
        ),
        cost_estimate=pl.CostEstimate(
            flops=9_000_000_000, bytes_accessed=12 << 20, transcendentals=0
        ),
    )(meta, incoming, slope1, slope0, kernel1, acts0)


SG = 2


def spread_kernel(
    corner_ref, p_ref, off_ref, k_ref, tl_ref, tr_ref, bl_ref, br_ref, held, row_w, weight, total
):
    step = pl.program_id(0)

    @pl.when(step == 0)
    def _():
        clear_edges(held, SG)
        total[...] = jnp.zeros_like(total)

    for g in range(SG):
        hold(held, g, p_ref[g].astype(F32))
    row_at = 4.0 * lax.broadcasted_iota(jnp.int32, (BOX, C), 0).astype(F32)
    col_at = 4.0 * lax.broadcasted_iota(jnp.int32, (SPAN, C), 0).astype(F32)
    for g in range(SG):
        row_w[g] = tent(row_at, off_ref[g, 0:1, :])
        col_w = tent(col_at, off_ref[g, 1:2, :])
        for p in range(BOX):
            weight[g, p * SPAN : (p + 1) * SPAN, :] = (row_w[g, p : p + 1, :] * col_w).astype(BF)
    for g in range(SG):
        slot = step * SG + g
        top = corner_ref[slot, 0]
        left = pl.multiple_of(corner_ref[slot, 1] // 16 * 16, 16)
        grad = jnp.concatenate([input_grad(held, g, k_ref), jnp.zeros((C - PIX, C), BF)], axis=0)
        for part in range(4):
            at = part * (BOX // 4)
            spread = dot(weight[g, at * SPAN : (at + BOX // 4) * SPAN, :], grad)
            total[pl.ds(top + at, BOX // 4), pl.ds(left, SPAN), :] += spread.reshape(
                BOX // 4, SPAN, C
            )

    @pl.when(step == pl.num_programs(0) - 1)
    def _():
        tl_ref[...] = total[0:BOX, 0:BOX, :]
        tr_ref[...] = total[0:BOX, BOX : 2 * BOX, :].astype(BF)
        bl_ref[...] = total[BOX : 2 * BOX, 0:BOX, :].astype(BF)
        br_ref[...] = total[BOX : 2 * BOX, BOX : 2 * BOX, :].astype(BF)


def spread(corners, inner, off_rows, kernel0):
    slots = corners.shape[0]
    whole = lambda *shape: pl.BlockSpec(shape, lambda i, *_: (0,) * len(shape))
    piece = lambda kind: jax.ShapeDtypeStruct((BOX, BOX, C), kind)
    return pl.pallas_call(
        spread_kernel,
        name="spread",
        out_shape=[piece(F32), piece(BF), piece(BF), piece(BF)],
        grid_spec=pltpu.PrefetchScalarGridSpec(
            num_scalar_prefetch=1,
            grid=(slots // SG,),
            in_specs=[
                pl.BlockSpec((SG, PIX, C), lambda i, *_: (i, 0, 0)),
                pl.BlockSpec((SG, 8, C), lambda i, *_: (i, 0, 0)),
                whole(9, C, C),
            ],
            out_specs=[whole(BOX, BOX, C)] * 4,
            scratch_shapes=[
                pltpu.VMEM((3, SG, ROWS, C), BF),
                pltpu.VMEM((SG, BOX, C), F32),
                pltpu.VMEM((SG, WIN, C), BF),
                pltpu.VMEM((2 * BOX, 2 * BOX, C), F32),
            ],
        ),
        cost_estimate=pl.CostEstimate(
            flops=7_000_000_000, bytes_accessed=6 << 20, transcendentals=0
        ),
    )(corners, inner, off_rows, kernel0)


def swap_cores(x):
    return lax.ppermute(x, "ha", [(i, i ^ 1) for i in range(lax.axis_size("ha"))])


def sum_everywhere(grads):
    core = lax.axis_index("ha") % 2
    rows = grads.shape[0] // 2
    mine = lax.dynamic_slice_in_dim(grads, core * rows, rows)
    other = lax.dynamic_slice_in_dim(grads, (1 - core) * rows, rows)
    half = (mine.astype(F32) + swap_cores(other).astype(F32)).astype(BF)
    peers = lax.axis_size("wa")
    parts = lax.all_to_all(half.reshape(peers, rows // peers, C), "wa", 0, 0, tiled=True)
    part = jnp.sum(parts.astype(F32), axis=0).astype(BF)
    total = part.astype(F32)
    count = lax.axis_size("ha")
    for hop in range(2, count, 2):
        moved = lax.ppermute(part, "ha", [(i, (i + hop) % count) for i in range(count)])
        total = total + moved.astype(F32)
    whole = jnp.broadcast_to(total.astype(BF)[None], (peers, *total.shape))
    half = lax.all_to_all(whole, "wa", 0, 0, tiled=True).reshape(rows, C)
    other = swap_cores(half)
    return jnp.where(
        core == 0, jnp.concatenate([half, other]), jnp.concatenate([other, half])
    ).astype(F32)


def local(features, counts, owner_perm, corners, offsets, kernels, cotangent):
    slots = corners.shape[0]
    peers = lax.axis_size("wa")
    col_index = lax.axis_index("wa")
    chunks = 4
    rows = BOX // chunks
    cut = lambda x: [x[rows * k : rows * (k + 1)] for k in range(chunks)]
    from_right = [shifted(piece, "wa", -1) for piece in cut(features)]
    below = shifted(features, "ha", -1)
    corner = [shifted(piece, "ha", -1) for piece in from_right]
    pieces = (features, jnp.concatenate(from_right), below, jnp.concatenate(corner))
    row_counts = lax.all_to_all(
        jnp.broadcast_to(counts[None], (peers, 1, 1)), "wa", 0, 0, tiled=True
    ).reshape(peers)
    ids = jnp.arange(peers, dtype=jnp.int32)
    starts = jnp.sum(jnp.where(ids[None, :] < ids[:, None], row_counts[None, :], 0), axis=1)
    here_start = jnp.sum(jnp.where(ids == col_index, starts, 0))
    perm_row = owner_perm[0]
    position = jnp.sum(jnp.where(perm_row == col_index, ids, 0))
    arrival = starts + (position - starts) % peers
    index = jnp.clip(arrival // peers, 0, cotangent.shape[0] - 1).astype(jnp.int32)
    stream = (here_start + ids) % peers
    owner_of = jnp.sum(jnp.where(stream[:, None] == ids[None, :], perm_row[None, :], 0), axis=1)
    meta = jnp.concatenate([owner_of, counts[0]]).astype(jnp.int32)
    outgoing = route(index, cotangent).reshape(peers, PIX, C)
    incoming = lax.all_to_all(outgoing, "wa", split_axis=0, concat_axis=0, tiled=True)
    shift = (corners[:, 1:2] % 16) * 4
    row_off = offsets[:, :SIDE].astype(F32)
    col_off = (offsets[:, SIDE:] + shift).astype(F32)
    pad = lambda x, n: jnp.pad(x, ((0, 0), (0, n)), constant_values=-1000.0)
    both = jnp.concatenate([pad(row_off, 2), pad(col_off, 2)], axis=1)
    off_cols = jnp.broadcast_to(both[:, :, None], (slots, 32, 128))
    row_lanes = pad(jnp.repeat(row_off, PITCH, axis=1), C - PIX)
    col_lanes = pad(jnp.tile(pad(col_off, 2), (1, SIDE)), C - PIX)
    off_rows = jnp.broadcast_to(
        jnp.stack([row_lanes, col_lanes], axis=1)[:, None], (slots, 4, 2, C)
    ).reshape(slots, 8, C)
    at = jnp.arange(WIN, dtype=jnp.int32)
    places = jnp.broadcast_to(
        jnp.stack([4 * (at // SPAN), 4 * (at % SPAN)])[None], (4, 2, WIN)
    ).reshape(8, WIN).astype(F32)
    taps = kernels.reshape(2, 9, C, C)
    acts0, acts1, slope0, slope1 = forward(corners, pieces, off_cols, places, taps)
    grad1 = last_grad(meta, incoming, slope1, acts1)
    inner, grad0 = middle_grad(meta, incoming, slope1, slope0, taps[1], acts0)
    grads = sum_everywhere(jnp.concatenate([grad0, grad1]).reshape(-1, C))
    tile, right, lower, corner = spread(corners, inner, off_rows, taps[0])
    parts = []
    for own, piece in zip(cut(right), cut(corner)):
        moved = shifted(piece, "ha", 1)
        parts.append(shifted((own.astype(F32) + moved.astype(F32)).astype(BF), "wa", 1))
    from_above = shifted(lower, "ha", 1)
    tile = tile + from_above.astype(F32) + jnp.concatenate(parts).astype(F32)
    return (tile, grads.reshape(2, 3, 3, C, C))


def solution(mesh):
    in_specs = (
        P("ha", "wa", None),
        P("ha", "wa"),
        P("ha", None),
        P(("ha", "wa"), None),
        P(("ha", "wa"), None),
        P(),
        P(("ha", "wa"), None, None, None),
    )
    out_specs = (P("ha", "wa", None), P())
    return jax.shard_map(local, mesh=mesh, in_specs=in_specs, out_specs=out_specs, check_vma=False)
```

```python
import functools

import jax
import jax.numpy as jnp
from jax import lax
from jax.experimental import pallas as pl
from jax.experimental.pallas import tpu as pltpu
from jax.sharding import PartitionSpec as P

SIDE = 14
PITCH = 16
PIX = SIDE * PITCH
BOX = 32
SPAN = 48
WIN = BOX * SPAN
ROWS = 288
C = 256
BF = jnp.bfloat16
F32 = jnp.float32


def shifted(value, axis, steps):
    count = lax.axis_size(axis)
    first, last = (max(0, -steps), min(count, count - steps))
    return lax.ppermute(value, axis, [(source, source + steps) for source in range(first, last)])


def dot(a, b, dims=(((1,), (0,)), ((), ()))):
    return lax.dot_general(a, b, dims, preferred_element_type=F32)


def inside(rows):
    pixel = lax.broadcasted_iota(jnp.int32, (rows, C), 0)
    return (pixel & (PITCH - 1)) < SIDE


def clear_edges(held, copies):
    for shift in range(3):
        for g in range(copies):
            held[shift, g, 0:16, :] = jnp.zeros((16, C), BF)
            held[shift, g, 16 + PIX : ROWS, :] = jnp.zeros((ROWS - 16 - PIX, C), BF)


def hold(held, g, value):
    held[0, g, 16 : 16 + PIX, :] = pltpu.roll(value, 1, 0).astype(BF)
    held[1, g, 16 : 16 + PIX, :] = value.astype(BF)
    held[2, g, 16 : 16 + PIX, :] = pltpu.roll(value, PIX - 1, 0).astype(BF)


def tent(places, offsets):
    return jnp.maximum(0.0, 1.0 - jnp.abs(places - offsets) * 0.25)


def gelu_parts(v):
    cdf = 0.5 * (1.0 + lax.erf(v * 0.7071067811865476))
    slope = cdf + v * (jnp.exp(v * v * -0.5) * 0.3989422804014327)
    return v * cdf, slope


def route_kernel(count_ref, perm_ref, x_ref, o_ref, meta_ref):
    peers = o_ref.shape[0]
    here = lax.axis_index("wa")
    position = jnp.int32(0)
    for i in range(peers):
        position = jnp.where(perm_ref[0, i] == here, i, position)
    start = jnp.int32(0)
    here_start = jnp.int32(0)
    gap = jnp.zeros((SIDE, PITCH - SIDE, C), BF)
    for i in range(peers):
        here_start = jnp.where(here == i, start, here_start)
        arrival = start + ((position - start) & (peers - 1))
        region = jnp.clip(arrival // peers, 0, x_ref.shape[0] - 1)
        o_ref[i, :, 0:SIDE, :] = x_ref[region]
        o_ref[i, :, SIDE:PITCH, :] = gap
        start = start + count_ref[i]
    for i in range(peers):
        meta_ref[i] = perm_ref[0, (here_start + i) & (peers - 1)]
    meta_ref[peers] = count_ref[here]


def route(counts, perm, cotangent):
    peers = counts.shape[0]
    smem = pl.BlockSpec(memory_space=pltpu.SMEM)
    vmem = pl.BlockSpec(memory_space=pltpu.VMEM)
    return pl.pallas_call(
        route_kernel,
        name="route",
        out_shape=[
            jax.ShapeDtypeStruct((peers, SIDE, PITCH, C), BF),
            jax.ShapeDtypeStruct((peers + 1,), jnp.int32),
        ],
        in_specs=[smem, smem, vmem],
        out_specs=[vmem, smem],
        cost_estimate=pl.CostEstimate(flops=0, bytes_accessed=4 << 20, transcendentals=0),
    )(counts, perm, cotangent)


FG = 4


def forward_kernel(
    corner_ref, tl_ref, tr0_ref, tr1_ref, bl_ref, br0_ref, br1_ref, off_ref, k_ref,
    a0_ref, a1_ref, g0_ref, g1_ref, t_ref, ext, places, row_w, weight, held,
):
    step = pl.program_id(0)
    half = BOX // 2

    @pl.when(step == 0)
    def _():
        clear_edges(held, FG)
        ext[0:BOX, 0:BOX, :] = tl_ref[...]
        ext[0:half, BOX : 2 * BOX, :] = tr0_ref[...]
        ext[half:BOX, BOX : 2 * BOX, :] = tr1_ref[...]
        ext[BOX : 2 * BOX, 0:BOX, :] = bl_ref[...]
        ext[BOX : BOX + half, BOX : 2 * BOX, :] = br0_ref[...]
        ext[BOX + half : 2 * BOX, BOX : 2 * BOX, :] = br1_ref[...]
        at = lax.broadcasted_iota(jnp.int32, (16, WIN), 1).astype(F32)
        row = jnp.floor((at + 0.5) * (1.0 / SPAN))
        places[0] = 4.0 * row
        places[1] = 4.0 * (at - SPAN * row)

    keep = inside(PIX)
    lane = lax.broadcasted_iota(jnp.int32, (32, 128), 1)
    for g in range(FG):
        slot = step * FG + g
        top = corner_ref[slot]
        left = pl.multiple_of(corner_ref[16 + slot] // 16 * 16, 16)
        offsets = jnp.sum(jnp.where(lane == slot, off_ref[...], 0.0), axis=1, keepdims=True)
        row_w[g] = tent(places[0], offsets[0:16])
        col_w = tent(places[1], offsets[16:32])
        for i in range(SIDE):
            weight[g, i * PITCH : (i + 1) * PITCH, :] = (row_w[g, i : i + 1, :] * col_w).astype(BF)
        window = ext[pl.ds(top, BOX), pl.ds(left, SPAN), :].reshape(WIN, C)
        hold(held, g, dot(weight[g], window))
        a0_ref[:, g * C : (g + 1) * C] = held[1, g, 16 : 16 + C, :].T
    for i in range(5):
        tap = jnp.minimum(step * 5 + i, 17)
        t_ref[tap] = k_ref[tap].T
    for layer in range(2):
        for g in range(FG):
            pre = jnp.zeros((PIX, C), F32)
            for dy in range(3):
                for dx in range(3):
                    pre += dot(held[dx, g, 16 * dy : 16 * dy + PIX, :], k_ref[layer * 9 + dy * 3 + dx])
            value, slope = gelu_parts(pre)
            slope = jnp.where(keep, slope, 0.0).astype(BF)
            if layer == 0:
                g0_ref[g] = slope
                hold(held, g, jnp.where(keep, value, 0.0))
                a1_ref[:, g * C : (g + 1) * C] = held[1, g, 16 : 16 + C, :].T
            else:
                g1_ref[g] = slope


def forward(corners, pieces, offsets, kernels):
    slots = 16
    half = BOX // 2
    whole = lambda *shape: pl.BlockSpec(shape, lambda i, *_: (0,) * len(shape))
    columns = pl.BlockSpec((C, FG * C), lambda i, *_: (0, i))
    regions = pl.BlockSpec((FG, PIX, C), lambda i, *_: (i, 0, 0))
    return pl.pallas_call(
        forward_kernel,
        name="forward",
        out_shape=[
            jax.ShapeDtypeStruct((C, slots * C), BF),
            jax.ShapeDtypeStruct((C, slots * C), BF),
            jax.ShapeDtypeStruct((slots, PIX, C), BF),
            jax.ShapeDtypeStruct((slots, PIX, C), BF),
            jax.ShapeDtypeStruct((18, C, C), BF),
        ],
        grid_spec=pltpu.PrefetchScalarGridSpec(
            num_scalar_prefetch=1,
            grid=(slots // FG,),
            in_specs=[
                whole(BOX, BOX, C),
                whole(half, BOX, C),
                whole(half, BOX, C),
                whole(BOX, BOX, C),
                whole(half, BOX, C),
                whole(half, BOX, C),
                whole(32, 128),
                whole(18, C, C),
            ],
            out_specs=[columns, columns, regions, regions, whole(18, C, C)],
            scratch_shapes=[
                pltpu.VMEM((2 * BOX, 2 * BOX, C), BF),
                pltpu.VMEM((2, 16, WIN), F32),
                pltpu.VMEM((FG, 16, WIN), F32),
                pltpu.VMEM((FG, PIX, WIN), BF),
                pltpu.VMEM((3, FG, ROWS, C), BF),
            ],
        ),
        cost_estimate=pl.CostEstimate(
            flops=11_300_000_000, bytes_accessed=14 << 20, transcendentals=4_000_000
        ),
    )(corners, *pieces, offsets, kernels)


BG = 4


def top_grad(meta_ref, slot, in_ref, g1_ref, g):
    source = meta_ref[slot]
    live = slot < meta_ref[16]
    grad = in_ref[source].astype(F32) * g1_ref[g].astype(F32)
    return jnp.where(live, grad, 0.0)


def kernel_grad(step, steps, held, a_ref, acc, o_ref):
    @pl.when(step == 0)
    def _():
        acc[...] = jnp.zeros_like(acc)

    for dy in range(3):
        for dx in range(3):
            grads = held[2 - dx, :, 32 - 16 * dy : 32 - 16 * dy + C, :].reshape(BG * C, C)
            acc[dy * 3 + dx] += dot(a_ref[...], grads)

    @pl.when(step == steps - 1)
    def _():
        o_ref[...] = acc[...].astype(BF)


def last_kernel(meta_ref, in_ref, g1_ref, a_ref, o_ref, held, acc):
    step = pl.program_id(0)

    @pl.when(step == 0)
    def _():
        clear_edges(held, BG)

    for g in range(BG):
        hold(held, g, top_grad(meta_ref, step * BG + g, in_ref, g1_ref, g))
    kernel_grad(step, pl.num_programs(0), held, a_ref, acc, o_ref)


def last_grad(meta, incoming, slope1, acts1):
    slots = slope1.shape[0]
    return pl.pallas_call(
        last_kernel,
        name="last_grad",
        out_shape=jax.ShapeDtypeStruct((9, C, C), BF),
        grid_spec=pltpu.PrefetchScalarGridSpec(
            num_scalar_prefetch=1,
            grid=(slots // BG,),
            in_specs=[
                pl.BlockSpec((16, PIX, C), lambda i, *_: (0, 0, 0)),
                pl.BlockSpec((BG, PIX, C), lambda i, *_: (i, 0, 0)),
                pl.BlockSpec((C, BG * C), lambda i, *_: (0, i)),
            ],
            out_specs=pl.BlockSpec((9, C, C), lambda i, *_: (0, 0, 0)),
            scratch_shapes=[pltpu.VMEM((3, BG, ROWS, C), BF), pltpu.VMEM((9, C, C), F32)],
        ),
        cost_estimate=pl.CostEstimate(
            flops=4_800_000_000, bytes_accessed=8 << 20, transcendentals=0
        ),
    )(meta, incoming, slope1, acts1)


def input_grad(held, g, k_ref):
    total = jnp.zeros((PIX, C), F32)
    for dy in range(3):
        for dx in range(3):
            total += dot(
                held[2 - dx, g, 32 - 16 * dy : 32 - 16 * dy + PIX, :],
                k_ref[dy * 3 + dx],
            )
    return total.astype(BF)


def middle_kernel(
    meta_ref, in_ref, g1_ref, g0_ref, k_ref, a_ref, p_ref, o_ref, upper, held, acc
):
    step = pl.program_id(0)

    @pl.when(step == 0)
    def _():
        clear_edges(upper, BG)
        clear_edges(held, BG)

    for g in range(BG):
        hold(upper, g, top_grad(meta_ref, step * BG + g, in_ref, g1_ref, g))
    for g in range(BG):
        grad = input_grad(upper, g, k_ref).astype(F32) * g0_ref[g].astype(F32)
        p_ref[g] = grad.astype(BF)
        hold(held, g, grad)
    kernel_grad(step, pl.num_programs(0), held, a_ref, acc, o_ref)


def middle_grad(meta, incoming, slope1, slope0, kernels, acts0):
    slots = slope1.shape[0]
    return pl.pallas_call(
        middle_kernel,
        name="middle_grad",
        out_shape=[
            jax.ShapeDtypeStruct((slots, PIX, C), BF),
            jax.ShapeDtypeStruct((9, C, C), BF),
        ],
        grid_spec=pltpu.PrefetchScalarGridSpec(
            num_scalar_prefetch=1,
            grid=(slots // BG,),
            in_specs=[
                pl.BlockSpec((16, PIX, C), lambda i, *_: (0, 0, 0)),
                pl.BlockSpec((BG, PIX, C), lambda i, *_: (i, 0, 0)),
                pl.BlockSpec((BG, PIX, C), lambda i, *_: (i, 0, 0)),
                pl.BlockSpec((9, C, C), lambda i, *_: (1, 0, 0)),
                pl.BlockSpec((C, BG * C), lambda i, *_: (0, i)),
            ],
            out_specs=[
                pl.BlockSpec((BG, PIX, C), lambda i, *_: (i, 0, 0)),
                pl.BlockSpec((9, C, C), lambda i, *_: (0, 0, 0)),
            ],
            scratch_shapes=[
                pltpu.VMEM((3, BG, ROWS, C), BF),
                pltpu.VMEM((3, BG, ROWS, C), BF),
                pltpu.VMEM((9, C, C), F32),
            ],
        ),
        cost_estimate=pl.CostEstimate(
            flops=9_000_000_000, bytes_accessed=12 << 20, transcendentals=0
        ),
    )(meta, incoming, slope1, slope0, kernels, acts0)


SG = 4
PART = 4


def spread_kernel(
    corner_ref, p_ref, off_ref, k_ref, tl_ref, tr_ref, bl_ref, br_ref, held, row_w, lanes, total
):
    step = pl.program_id(0)

    @pl.when(step == 0)
    def _():
        clear_edges(held, SG)
        total[...] = jnp.zeros_like(total)
        entry = lax.broadcasted_iota(jnp.int32, (32, C), 0)
        pixel = lax.broadcasted_iota(jnp.int32, (32, C), 1)
        for axis in range(2):
            index = pixel // PITCH if axis == 0 else 16 + (pixel & (PITCH - 1))
            pick = jnp.where(entry == index, 1.0, 0.0).astype(BF)
            lanes[axis] = dot(off_ref[...].astype(BF), pick)

    for g in range(SG):
        hold(held, g, p_ref[g].astype(F32))
    row_at = 4.0 * lax.broadcasted_iota(jnp.int32, (BOX, C), 0).astype(F32)
    col_at = 4.0 * lax.broadcasted_iota(jnp.int32, (SPAN, C), 0).astype(F32)
    grads = [
        jnp.concatenate([input_grad(held, g, k_ref), jnp.zeros((C - PIX, C), BF)], axis=0)
        for g in range(SG)
    ]
    for g in range(SG):
        slot = step * SG + g
        top = corner_ref[slot]
        left = pl.multiple_of(corner_ref[16 + slot] // 16 * 16, 16)
        row_w[g] = tent(row_at, lanes[0, pl.ds(slot, 1), :])
        col_w = tent(col_at, lanes[1, pl.ds(slot, 1), :])
        for at in range(0, BOX, PART):
            weight = jnp.concatenate(
                [(row_w[g, p : p + 1, :] * col_w).astype(BF) for p in range(at, at + PART)], axis=0
            )
            total[pl.ds(top + at, PART), pl.ds(left, SPAN), :] += dot(weight, grads[g]).reshape(
                PART, SPAN, C
            )

    @pl.when(step == pl.num_programs(0) - 1)
    def _():
        tl_ref[...] = total[0:BOX, 0:BOX, :]
        tr_ref[...] = total[0:BOX, BOX : 2 * BOX, :].astype(BF)
        bl_ref[...] = total[BOX : 2 * BOX, 0:BOX, :].astype(BF)
        br_ref[...] = total[BOX : 2 * BOX, BOX : 2 * BOX, :].astype(BF)


def spread(corners, inner, offsets, kernels):
    slots = inner.shape[0]
    whole = lambda *shape: pl.BlockSpec(shape, lambda i, *_: (0,) * len(shape))
    piece = lambda kind: jax.ShapeDtypeStruct((BOX, BOX, C), kind)
    return pl.pallas_call(
        spread_kernel,
        name="spread",
        out_shape=[piece(F32), piece(BF), piece(BF), piece(BF)],
        grid_spec=pltpu.PrefetchScalarGridSpec(
            num_scalar_prefetch=1,
            grid=(slots // SG,),
            in_specs=[
                pl.BlockSpec((SG, PIX, C), lambda i, *_: (i, 0, 0)),
                whole(16, 32),
                whole(9, C, C),
            ],
            out_specs=[whole(BOX, BOX, C)] * 4,
            scratch_shapes=[
                pltpu.VMEM((3, SG, ROWS, C), BF),
                pltpu.VMEM((SG, BOX, C), F32),
                pltpu.VMEM((2, 16, C), F32),
                pltpu.VMEM((2 * BOX, 2 * BOX, C), F32),
            ],
        ),
        cost_estimate=pl.CostEstimate(
            flops=7_000_000_000, bytes_accessed=6 << 20, transcendentals=0
        ),
    )(corners, inner, offsets, kernels)


def swap_cores(x):
    return lax.ppermute(x, "ha", [(i, i ^ 1) for i in range(lax.axis_size("ha"))])


def pick_layer(index, first, second):
    return jnp.where(index == 0, first, second)


def local(features, counts, owner_perm, corners, offsets, kernels, cotangent):
    peers = lax.axis_size("wa")
    core = lax.axis_index("ha") % 2
    rows = BOX // 2
    cut = lambda x: (x[:rows], x[rows:])
    row_counts = lax.all_to_all(
        jnp.broadcast_to(counts[None], (peers, 1, 1)), "wa", 0, 0, tiled=True
    ).reshape(peers)
    features, row_counts = lax.optimization_barrier((features, row_counts))
    from_right = [shifted(piece, "wa", -1) for piece in cut(features)]
    below = shifted(features, "ha", -1)
    outgoing, meta = route(row_counts, owner_perm, cotangent)
    incoming = lax.all_to_all(
        outgoing.reshape(peers, PIX, C), "wa", split_axis=0, concat_axis=0, tiled=True
    )
    corner = [shifted(piece, "ha", -1) for piece in from_right]
    pieces = (features, *from_right, below, *corner)
    places = jnp.concatenate(
        [offsets[:, :SIDE], offsets[:, SIDE:] + (corners[:, 1:2] % 16) * 4], axis=1
    ).astype(F32)
    pad = lambda x: jnp.pad(x, ((0, 0), (0, 2)), constant_values=-1000.0)
    places = jnp.concatenate([pad(places[:, :SIDE]), pad(places[:, SIDE:])], axis=1)
    place_cols = jnp.pad(places.T, ((0, 0), (0, 112)))
    corners = corners.T.reshape(-1)
    acts0, acts1, slope0, slope1, turned = forward(
        corners, pieces, place_cols, kernels.reshape(18, C, C)
    )
    grad1 = last_grad(meta, incoming, slope1, acts1)
    inner, grad0 = middle_grad(meta, incoming, slope1, slope0, turned, acts0)
    mine = swap_cores(pick_layer(core, grad1, grad0)).astype(F32)
    mine = (mine + pick_layer(core, grad0, grad1).astype(F32)).astype(BF)
    parts = lax.all_to_all(mine.reshape(peers, -1, C), "wa", 0, 0, tiled=True)
    tile, right, lower, corner = spread(corners, inner, places, turned)
    parts, tile, right, lower, corner = lax.optimization_barrier(
        (parts, tile, right, lower, corner)
    )
    part = jnp.sum(parts.astype(F32), axis=0).astype(BF)
    count = lax.axis_size("ha")
    total = part.astype(F32)
    for hop in range(2, count, 2):
        moved = lax.ppermute(part, "ha", [(i, (i + hop) % count) for i in range(count)])
        total = total + moved.astype(F32)
    whole = jnp.broadcast_to(total.astype(BF)[None], (peers, *total.shape))
    mine = lax.all_to_all(whole, "wa", 0, 0, tiled=True).reshape(9, C, C)
    sides = []
    for own, piece in zip(cut(right), cut(corner)):
        moved = shifted(piece, "ha", 1)
        sides.append(shifted((own.astype(F32) + moved.astype(F32)).astype(BF), "wa", 1))
    from_above = shifted(lower, "ha", 1)
    mine, from_above, *sides = lax.optimization_barrier((mine, from_above, *sides))
    tile = tile + from_above.astype(F32) + jnp.concatenate(sides).astype(F32)
    other = swap_cores(mine)
    grads = jnp.stack([pick_layer(core, mine, other), pick_layer(core, other, mine)]).astype(F32)
    return (tile, grads.reshape(2, 3, 3, C, C))


def solution(mesh):
    in_specs = (
        P("ha", "wa", None),
        P("ha", "wa"),
        P("ha", None),
        P(("ha", "wa"), None),
        P(("ha", "wa"), None),
        P(),
        P(("ha", "wa"), None, None, None),
    )
    out_specs = (P("ha", "wa", None), P())
    return jax.shard_map(local, mesh=mesh, in_specs=in_specs, out_specs=out_specs, check_vma=False)
```

```python
import jax
import jax.numpy as jnp
from jax import lax
from jax.experimental import pallas as pl
from jax.experimental.pallas import tpu as pltpu
from jax.sharding import PartitionSpec as P

SIDE = 14
PITCH = 16
PIX = SIDE * PITCH
BOX = 32
SPAN = 48
WIN = BOX * SPAN
ROWS = 288
C = 256
BF = jnp.bfloat16
F32 = jnp.float32


def shifted(value, axis, steps):
    count = lax.axis_size(axis)
    first, last = (max(0, -steps), min(count, count - steps))
    return lax.ppermute(value, axis, [(source, source + steps) for source in range(first, last)])


def dot(a, b, dims=(((1,), (0,)), ((), ()))):
    return lax.dot_general(a, b, dims, preferred_element_type=F32)


def inside(rows):
    pixel = lax.broadcasted_iota(jnp.int32, (rows, C), 0)
    return (pixel & (PITCH - 1)) < SIDE


def clear_edges(held, copies):
    for shift in range(3):
        for g in range(copies):
            held[shift, g, 0:16, :] = jnp.zeros((16, C), BF)
            held[shift, g, 16 + PIX : ROWS, :] = jnp.zeros((ROWS - 16 - PIX, C), BF)


def hold(held, g, value):
    held[0, g, 16 : 16 + PIX, :] = pltpu.roll(value, 1, 0).astype(BF)
    held[1, g, 16 : 16 + PIX, :] = value.astype(BF)
    held[2, g, 16 : 16 + PIX, :] = pltpu.roll(value, PIX - 1, 0).astype(BF)


def tent(places, offsets):
    return jnp.maximum(0.0, 1.0 - jnp.abs(places - offsets) * 0.25)


def gelu_parts(v):
    cdf = 0.5 * (1.0 + lax.erf(v * 0.7071067811865476))
    slope = cdf + v * (jnp.exp(v * v * -0.5) * 0.3989422804014327)
    return v * cdf, slope


def route_kernel(count_ref, perm_ref, x_ref, o_ref, meta_ref):
    peers = o_ref.shape[0]
    here = lax.axis_index("wa")
    position = jnp.int32(0)
    for i in range(peers):
        position = jnp.where(perm_ref[0, i] == here, i, position)
    start = jnp.int32(0)
    here_start = jnp.int32(0)
    gap = jnp.zeros((SIDE, PITCH - SIDE, C), BF)
    for i in range(peers):
        here_start = jnp.where(here == i, start, here_start)
        arrival = start + ((position - start) & (peers - 1))
        region = jnp.clip(arrival // peers, 0, x_ref.shape[0] - 1)
        o_ref[i, :, 0:SIDE, :] = x_ref[region]
        o_ref[i, :, SIDE:PITCH, :] = gap
        start = start + count_ref[i]
    for i in range(peers):
        meta_ref[i] = perm_ref[0, (here_start + i) & (peers - 1)]
    meta_ref[peers] = count_ref[here]


def route(counts, perm, cotangent):
    peers = counts.shape[0]
    smem = pl.BlockSpec(memory_space=pltpu.SMEM)
    vmem = pl.BlockSpec(memory_space=pltpu.VMEM)
    return pl.pallas_call(
        route_kernel,
        name="route",
        out_shape=[
            jax.ShapeDtypeStruct((peers, SIDE, PITCH, C), BF),
            jax.ShapeDtypeStruct((peers + 1,), jnp.int32),
        ],
        in_specs=[smem, smem, vmem],
        out_specs=[vmem, smem],
        cost_estimate=pl.CostEstimate(flops=0, bytes_accessed=4 << 20, transcendentals=0),
    )(counts, perm, cotangent)


FG = 4


def forward_kernel(
    corner_ref, tl_ref, tr0_ref, tr1_ref, bl_ref, br0_ref, br1_ref, off_ref, k_ref,
    a0_ref, a1_ref, g0_ref, g1_ref, t_ref, ext, places, row_w, weight, held,
):
    step = pl.program_id(0)
    half = BOX // 2

    @pl.when(step == 0)
    def _():
        clear_edges(held, FG)
        ext[0:BOX, 0:BOX, :] = tl_ref[...]
        ext[0:half, BOX : 2 * BOX, :] = tr0_ref[...]
        ext[half:BOX, BOX : 2 * BOX, :] = tr1_ref[...]
        ext[BOX : 2 * BOX, 0:BOX, :] = bl_ref[...]
        ext[BOX : BOX + half, BOX : 2 * BOX, :] = br0_ref[...]
        ext[BOX + half : 2 * BOX, BOX : 2 * BOX, :] = br1_ref[...]
        at = lax.broadcasted_iota(jnp.int32, (16, WIN), 1).astype(F32)
        row = jnp.floor((at + 0.5) * (1.0 / SPAN))
        places[0] = 4.0 * row
        places[1] = 4.0 * (at - SPAN * row)

    keep = inside(PIX)
    lane = lax.broadcasted_iota(jnp.int32, (32, 128), 1)
    for g in range(FG):
        slot = step * FG + g
        top = corner_ref[slot]
        left = pl.multiple_of(corner_ref[16 + slot] // 16 * 16, 16)
        offsets = jnp.sum(jnp.where(lane == slot, off_ref[...], 0.0), axis=1, keepdims=True)
        row_w[g] = tent(places[0], offsets[0:16])
        col_w = tent(places[1], offsets[16:32])
        for i in range(SIDE):
            weight[g, i * PITCH : (i + 1) * PITCH, :] = (row_w[g, i : i + 1, :] * col_w).astype(BF)
        window = ext[pl.ds(top, BOX), pl.ds(left, SPAN), :].reshape(WIN, C)
        hold(held, g, dot(weight[g], window))
        a0_ref[:, g * C : (g + 1) * C] = held[1, g, 16 : 16 + C, :].T
    for i in range(5):
        tap = jnp.minimum(step * 5 + i, 17)
        t_ref[tap] = k_ref[tap].T
    for layer in range(2):
        for g in range(FG):
            pre = jnp.zeros((PIX, C), F32)
            for dy in range(3):
                for dx in range(3):
                    pre += dot(held[dx, g, 16 * dy : 16 * dy + PIX, :], k_ref[layer * 9 + dy * 3 + dx])
            value, slope = gelu_parts(pre)
            slope = jnp.where(keep, slope, 0.0).astype(BF)
            if layer == 0:
                g0_ref[g] = slope
                hold(held, g, jnp.where(keep, value, 0.0))
                a1_ref[:, g * C : (g + 1) * C] = held[1, g, 16 : 16 + C, :].T
            else:
                g1_ref[g] = slope


def forward(corners, pieces, offsets, kernels):
    slots = 16
    half = BOX // 2
    whole = lambda *shape: pl.BlockSpec(shape, lambda i, *_: (0,) * len(shape))
    columns = pl.BlockSpec((C, FG * C), lambda i, *_: (0, i))
    regions = pl.BlockSpec((FG, PIX, C), lambda i, *_: (i, 0, 0))
    return pl.pallas_call(
        forward_kernel,
        name="forward",
        out_shape=[
            jax.ShapeDtypeStruct((C, slots * C), BF),
            jax.ShapeDtypeStruct((C, slots * C), BF),
            jax.ShapeDtypeStruct((slots, PIX, C), BF),
            jax.ShapeDtypeStruct((slots, PIX, C), BF),
            jax.ShapeDtypeStruct((18, C, C), BF),
        ],
        grid_spec=pltpu.PrefetchScalarGridSpec(
            num_scalar_prefetch=1,
            grid=(slots // FG,),
            in_specs=[
                whole(BOX, BOX, C),
                whole(half, BOX, C),
                whole(half, BOX, C),
                whole(BOX, BOX, C),
                whole(half, BOX, C),
                whole(half, BOX, C),
                whole(32, 128),
                whole(18, C, C),
            ],
            out_specs=[columns, columns, regions, regions, whole(18, C, C)],
            scratch_shapes=[
                pltpu.VMEM((2 * BOX, 2 * BOX, C), BF),
                pltpu.VMEM((2, 16, WIN), F32),
                pltpu.VMEM((FG, 16, WIN), F32),
                pltpu.VMEM((FG, PIX, WIN), BF),
                pltpu.VMEM((3, FG, ROWS, C), BF),
            ],
        ),
        cost_estimate=pl.CostEstimate(
            flops=11_300_000_000, bytes_accessed=14 << 20, transcendentals=4_000_000
        ),
    )(corners, *pieces, offsets, kernels)


BG = 4


def top_grad(meta_ref, slot, in_ref, g1_ref, g):
    source = meta_ref[slot]
    live = slot < meta_ref[16]
    grad = in_ref[source].astype(F32) * g1_ref[g].astype(F32)
    return jnp.where(live, grad, 0.0)


def kernel_grad(step, steps, held, a_ref, acc, o_ref):
    @pl.when(step == 0)
    def _():
        acc[...] = jnp.zeros_like(acc)

    for dy in range(3):
        for dx in range(3):
            grads = held[2 - dx, :, 32 - 16 * dy : 32 - 16 * dy + C, :].reshape(BG * C, C)
            acc[dy * 3 + dx] += dot(a_ref[...], grads)

    @pl.when(step == steps - 1)
    def _():
        o_ref[...] = acc[...].astype(BF)


def last_kernel(meta_ref, in_ref, g1_ref, a_ref, o_ref, held, acc):
    step = pl.program_id(0)

    @pl.when(step == 0)
    def _():
        clear_edges(held, BG)

    for g in range(BG):
        hold(held, g, top_grad(meta_ref, step * BG + g, in_ref, g1_ref, g))
    kernel_grad(step, pl.num_programs(0), held, a_ref, acc, o_ref)


def last_grad(meta, incoming, slope1, acts1):
    slots = slope1.shape[0]
    return pl.pallas_call(
        last_kernel,
        name="last_grad",
        out_shape=jax.ShapeDtypeStruct((9, C, C), BF),
        grid_spec=pltpu.PrefetchScalarGridSpec(
            num_scalar_prefetch=1,
            grid=(slots // BG,),
            in_specs=[
                pl.BlockSpec((16, PIX, C), lambda i, *_: (0, 0, 0)),
                pl.BlockSpec((BG, PIX, C), lambda i, *_: (i, 0, 0)),
                pl.BlockSpec((C, BG * C), lambda i, *_: (0, i)),
            ],
            out_specs=pl.BlockSpec((9, C, C), lambda i, *_: (0, 0, 0)),
            scratch_shapes=[pltpu.VMEM((3, BG, ROWS, C), BF), pltpu.VMEM((9, C, C), F32)],
        ),
        cost_estimate=pl.CostEstimate(
            flops=4_800_000_000, bytes_accessed=8 << 20, transcendentals=0
        ),
    )(meta, incoming, slope1, acts1)


def input_grad(held, g, k_ref):
    total = jnp.zeros((PIX, C), F32)
    for dy in range(3):
        for dx in range(3):
            total += dot(
                held[2 - dx, g, 32 - 16 * dy : 32 - 16 * dy + PIX, :],
                k_ref[dy * 3 + dx],
            )
    return total.astype(BF)


def middle_kernel(
    meta_ref, in_ref, g1_ref, g0_ref, k_ref, a_ref, p_ref, o_ref, upper, held, acc
):
    step = pl.program_id(0)

    @pl.when(step == 0)
    def _():
        clear_edges(upper, BG)
        clear_edges(held, BG)

    for g in range(BG):
        hold(upper, g, top_grad(meta_ref, step * BG + g, in_ref, g1_ref, g))
    for g in range(BG):
        grad = input_grad(upper, g, k_ref).astype(F32) * g0_ref[g].astype(F32)
        p_ref[g] = grad.astype(BF)
        hold(held, g, grad)
    kernel_grad(step, pl.num_programs(0), held, a_ref, acc, o_ref)


def middle_grad(meta, incoming, slope1, slope0, kernels, acts0):
    slots = slope1.shape[0]
    return pl.pallas_call(
        middle_kernel,
        name="middle_grad",
        out_shape=[
            jax.ShapeDtypeStruct((slots, PIX, C), BF),
            jax.ShapeDtypeStruct((9, C, C), BF),
        ],
        grid_spec=pltpu.PrefetchScalarGridSpec(
            num_scalar_prefetch=1,
            grid=(slots // BG,),
            in_specs=[
                pl.BlockSpec((16, PIX, C), lambda i, *_: (0, 0, 0)),
                pl.BlockSpec((BG, PIX, C), lambda i, *_: (i, 0, 0)),
                pl.BlockSpec((BG, PIX, C), lambda i, *_: (i, 0, 0)),
                pl.BlockSpec((9, C, C), lambda i, *_: (1, 0, 0)),
                pl.BlockSpec((C, BG * C), lambda i, *_: (0, i)),
            ],
            out_specs=[
                pl.BlockSpec((BG, PIX, C), lambda i, *_: (i, 0, 0)),
                pl.BlockSpec((9, C, C), lambda i, *_: (0, 0, 0)),
            ],
            scratch_shapes=[
                pltpu.VMEM((3, BG, ROWS, C), BF),
                pltpu.VMEM((3, BG, ROWS, C), BF),
                pltpu.VMEM((9, C, C), F32),
            ],
        ),
        cost_estimate=pl.CostEstimate(
            flops=9_000_000_000, bytes_accessed=12 << 20, transcendentals=0
        ),
    )(meta, incoming, slope1, slope0, kernels, acts0)


SG = 4
PART = 4


def spread_kernel(
    corner_ref, p_ref, off_ref, k_ref, tl_ref, tr_ref, bl_ref, br_ref, held, row_w, lanes, total
):
    step = pl.program_id(0)

    @pl.when(step == 0)
    def _():
        clear_edges(held, SG)
        total[...] = jnp.zeros_like(total)
        entry = lax.broadcasted_iota(jnp.int32, (32, C), 0)
        pixel = lax.broadcasted_iota(jnp.int32, (32, C), 1)
        for axis in range(2):
            index = pixel // PITCH if axis == 0 else 16 + (pixel & (PITCH - 1))
            pick = jnp.where(entry == index, 1.0, 0.0).astype(BF)
            lanes[axis] = dot(off_ref[...].astype(BF), pick)

    for g in range(SG):
        hold(held, g, p_ref[g].astype(F32))
    row_at = 4.0 * lax.broadcasted_iota(jnp.int32, (BOX, C), 0).astype(F32)
    col_at = 4.0 * lax.broadcasted_iota(jnp.int32, (SPAN, C), 0).astype(F32)
    grads = [
        jnp.concatenate([input_grad(held, g, k_ref), jnp.zeros((C - PIX, C), BF)], axis=0)
        for g in range(SG)
    ]
    for g in range(SG):
        slot = step * SG + g
        top = corner_ref[slot]
        left = pl.multiple_of(corner_ref[16 + slot] // 16 * 16, 16)
        row_w[g] = tent(row_at, lanes[0, pl.ds(slot, 1), :])
        col_w = tent(col_at, lanes[1, pl.ds(slot, 1), :])
        for at in range(0, BOX, PART):
            weight = jnp.concatenate(
                [(row_w[g, p : p + 1, :] * col_w).astype(BF) for p in range(at, at + PART)], axis=0
            )
            total[pl.ds(top + at, PART), pl.ds(left, SPAN), :] += dot(weight, grads[g]).reshape(
                PART, SPAN, C
            )

    @pl.when(step == pl.num_programs(0) - 1)
    def _():
        tl_ref[...] = total[0:BOX, 0:BOX, :]
        tr_ref[...] = total[0:BOX, BOX : 2 * BOX, :].astype(BF)
        bl_ref[...] = total[BOX : 2 * BOX, 0:BOX, :].astype(BF)
        br_ref[...] = total[BOX : 2 * BOX, BOX : 2 * BOX, :].astype(BF)


def spread(corners, inner, offsets, kernels):
    slots = inner.shape[0]
    whole = lambda *shape: pl.BlockSpec(shape, lambda i, *_: (0,) * len(shape))
    piece = lambda kind: jax.ShapeDtypeStruct((BOX, BOX, C), kind)
    return pl.pallas_call(
        spread_kernel,
        name="spread",
        out_shape=[piece(F32), piece(BF), piece(BF), piece(BF)],
        grid_spec=pltpu.PrefetchScalarGridSpec(
            num_scalar_prefetch=1,
            grid=(slots // SG,),
            in_specs=[
                pl.BlockSpec((SG, PIX, C), lambda i, *_: (i, 0, 0)),
                whole(16, 32),
                whole(9, C, C),
            ],
            out_specs=[whole(BOX, BOX, C)] * 4,
            scratch_shapes=[
                pltpu.VMEM((3, SG, ROWS, C), BF),
                pltpu.VMEM((SG, BOX, C), F32),
                pltpu.VMEM((2, 16, C), F32),
                pltpu.VMEM((2 * BOX, 2 * BOX, C), F32),
            ],
        ),
        cost_estimate=pl.CostEstimate(
            flops=7_000_000_000, bytes_accessed=6 << 20, transcendentals=0
        ),
    )(corners, inner, offsets, kernels)


def swap_cores(x):
    return lax.ppermute(x, "ha", [(i, i ^ 1) for i in range(lax.axis_size("ha"))])


def pick_layer(index, first, second):
    return jnp.where(index == 0, first, second)


def local(features, counts, owner_perm, corners, offsets, kernels, cotangent):
    peers = lax.axis_size("wa")
    core = lax.axis_index("ha") % 2
    rows = BOX // 2
    cut = lambda x: (x[:rows], x[rows:])
    row_counts = lax.all_to_all(
        jnp.broadcast_to(counts[None], (peers, 1, 1)), "wa", 0, 0, tiled=True
    ).reshape(peers)
    from_right = [shifted(piece, "wa", -1) for piece in cut(features)]
    below = shifted(features, "ha", -1)
    outgoing, meta = route(row_counts, owner_perm, cotangent)
    outgoing, from_right[0] = lax.optimization_barrier((outgoing, from_right[0]))
    corner = [shifted(piece, "ha", -1) for piece in from_right]
    incoming = lax.all_to_all(
        outgoing.reshape(peers, PIX, C), "wa", split_axis=0, concat_axis=0, tiled=True
    )
    pieces = (features, *from_right, below, *corner)
    places = jnp.concatenate(
        [offsets[:, :SIDE], offsets[:, SIDE:] + (corners[:, 1:2] % 16) * 4], axis=1
    ).astype(F32)
    pad = lambda x: jnp.pad(x, ((0, 0), (0, 2)), constant_values=-1000.0)
    places = jnp.concatenate([pad(places[:, :SIDE]), pad(places[:, SIDE:])], axis=1)
    place_cols = jnp.pad(places.T, ((0, 0), (0, 112)))
    corners = corners.T.reshape(-1)
    acts0, acts1, slope0, slope1, turned = forward(
        corners, pieces, place_cols, kernels.reshape(18, C, C)
    )
    grad1 = last_grad(meta, incoming, slope1, acts1)
    inner, grad0 = middle_grad(meta, incoming, slope1, slope0, turned, acts0)
    mine = swap_cores(pick_layer(core, grad1, grad0)).astype(F32)
    mine = (mine + pick_layer(core, grad0, grad1).astype(F32)).astype(BF)
    parts = lax.all_to_all(mine.reshape(peers, -1, C), "wa", 0, 0, tiled=True)
    tile, right, lower, corner = spread(corners, inner, places, turned)
    from_above = [shifted(piece, "ha", 1) for piece in (*cut(corner), lower)]
    part = jnp.sum(parts.astype(F32), axis=0).astype(BF)
    count = lax.axis_size("ha")
    sides = []
    for own, moved in zip(cut(right), from_above):
        sides.append(shifted((own.astype(F32) + moved.astype(F32)).astype(BF), "wa", 1))
    total = part.astype(F32)
    for hop in range(2, count, 2):
        moved = lax.ppermute(part, "ha", [(i, (i + hop) % count) for i in range(count)])
        total = total + moved.astype(F32)
    whole = jnp.broadcast_to(total.astype(BF)[None], (peers, *total.shape))
    mine = lax.all_to_all(whole, "wa", 0, 0, tiled=True).reshape(9, C, C)
    tile = tile + from_above[2].astype(F32)
    mine, tile, *sides = lax.optimization_barrier((mine, tile, *sides))
    tile = tile + jnp.concatenate(sides).astype(F32)
    other = swap_cores(mine)
    grads = jnp.stack([pick_layer(core, mine, other), pick_layer(core, other, mine)]).astype(F32)
    return (tile, grads.reshape(2, 3, 3, C, C))


def solution(mesh):
    in_specs = (
        P("ha", "wa", None),
        P("ha", "wa"),
        P("ha", None),
        P(("ha", "wa"), None),
        P(("ha", "wa"), None),
        P(),
        P(("ha", "wa"), None, None, None),
    )
    out_specs = (P("ha", "wa", None), P())

    return jax.shard_map(local, mesh=mesh, in_specs=in_specs, out_specs=out_specs, check_vma=False)
```

```python
import jax
import jax.numpy as jnp
from jax import lax
from jax.experimental import pallas as pl
from jax.experimental.pallas import tpu as pltpu
from jax.sharding import PartitionSpec as P

SIDE = 14
PITCH = 16
PIX = SIDE * PITCH
BOX = 32
SPAN = 48
WIN = BOX * SPAN
ROWS = 288
C = 256
BF = jnp.bfloat16
F32 = jnp.float32


def shifted(value, axis, steps):
    count = lax.axis_size(axis)
    first, last = (max(0, -steps), min(count, count - steps))
    return lax.ppermute(value, axis, [(source, source + steps) for source in range(first, last)])


def dot(a, b, dims=(((1,), (0,)), ((), ()))):
    return lax.dot_general(a, b, dims, preferred_element_type=F32)


def inside(rows):
    pixel = lax.broadcasted_iota(jnp.int32, (rows, C), 0)
    return (pixel & (PITCH - 1)) < SIDE


def clear_edges(held, copies):
    for shift in range(3):
        for g in range(copies):
            held[shift, g, 0:16, :] = jnp.zeros((16, C), BF)
            held[shift, g, 16 + PIX : ROWS, :] = jnp.zeros((ROWS - 16 - PIX, C), BF)


def hold(held, g, value):
    held[0, g, 16 : 16 + PIX, :] = pltpu.roll(value, 1, 0).astype(BF)
    held[1, g, 16 : 16 + PIX, :] = value.astype(BF)
    held[2, g, 16 : 16 + PIX, :] = pltpu.roll(value, PIX - 1, 0).astype(BF)


def tent(places, offsets):
    return jnp.maximum(0.0, 1.0 - jnp.abs(places - offsets) * 0.25)


def gelu_parts(v):
    cdf = 0.5 * (1.0 + lax.erf(v * 0.7071067811865476))
    slope = cdf + v * (jnp.exp(v * v * -0.5) * 0.3989422804014327)
    return v * cdf, slope


def route_kernel(count_ref, perm_ref, x_ref, o_ref, meta_ref):
    peers = o_ref.shape[0]
    here = lax.axis_index("wa")
    position = jnp.int32(0)
    for i in range(peers):
        position = jnp.where(perm_ref[0, i] == here, i, position)
    start = jnp.int32(0)
    here_start = jnp.int32(0)
    gap = jnp.zeros((SIDE, PITCH - SIDE, C), BF)
    for i in range(peers):
        here_start = jnp.where(here == i, start, here_start)
        arrival = start + ((position - start) & (peers - 1))
        region = jnp.clip(arrival // peers, 0, x_ref.shape[0] - 1)
        o_ref[i, :, 0:SIDE, :] = x_ref[region]
        o_ref[i, :, SIDE:PITCH, :] = gap
        start = start + count_ref[i]
    for i in range(peers):
        meta_ref[i] = perm_ref[0, (here_start + i) & (peers - 1)]
    meta_ref[peers] = count_ref[here]


def route(counts, perm, cotangent):
    peers = counts.shape[0]
    smem = pl.BlockSpec(memory_space=pltpu.SMEM)
    vmem = pl.BlockSpec(memory_space=pltpu.VMEM)
    return pl.pallas_call(
        route_kernel,
        name="route",
        out_shape=[
            jax.ShapeDtypeStruct((peers, SIDE, PITCH, C), BF),
            jax.ShapeDtypeStruct((peers + 1,), jnp.int32),
        ],
        in_specs=[smem, smem, vmem],
        out_specs=[vmem, smem],
        cost_estimate=pl.CostEstimate(flops=0, bytes_accessed=4 << 20, transcendentals=0),
    )(counts, perm, cotangent)


FG = 4


def forward_kernel(
    corner_ref, tl_ref, tr0_ref, tr1_ref, bl_ref, br0_ref, br1_ref, off_ref, k_ref,
    a0_ref, a1_ref, g0_ref, g1_ref, t_ref, ext, places, row_w, weight, held,
):
    step = pl.program_id(0)
    half = BOX // 2

    @pl.when(step == 0)
    def _():
        clear_edges(held, FG)
        ext[0:BOX, 0:BOX, :] = tl_ref[...]
        ext[0:half, BOX : 2 * BOX, :] = tr0_ref[...]
        ext[half:BOX, BOX : 2 * BOX, :] = tr1_ref[...]
        ext[BOX : 2 * BOX, 0:BOX, :] = bl_ref[...]
        ext[BOX : BOX + half, BOX : 2 * BOX, :] = br0_ref[...]
        ext[BOX + half : 2 * BOX, BOX : 2 * BOX, :] = br1_ref[...]
        at = lax.broadcasted_iota(jnp.int32, (16, WIN), 1).astype(F32)
        row = jnp.floor((at + 0.5) * (1.0 / SPAN))
        places[0] = 4.0 * row
        places[1] = 4.0 * (at - SPAN * row)

    keep = inside(PIX)
    lane = lax.broadcasted_iota(jnp.int32, (32, 16), 1)
    for g in range(FG):
        slot = step * FG + g
        top = corner_ref[slot]
        left = pl.multiple_of(corner_ref[16 + slot] // 16 * 16, 16)
        offsets = jnp.sum(jnp.where(lane == slot, off_ref[...], 0.0), axis=1, keepdims=True)
        row_w[g] = tent(places[0], offsets[0:16])
        col_w = tent(places[1], offsets[16:32])
        for i in range(SIDE):
            weight[g, i * PITCH : (i + 1) * PITCH, :] = (row_w[g, i : i + 1, :] * col_w).astype(BF)
        window = ext[pl.ds(top, BOX), pl.ds(left, SPAN), :].reshape(WIN, C)
        hold(held, g, dot(weight[g], window))
        a0_ref[:, g * C : (g + 1) * C] = held[1, g, 16 : 16 + C, :].T
    for i in range(5):
        tap = jnp.minimum(step * 5 + i, 17)
        t_ref[tap] = k_ref[tap].T
    for layer in range(2):
        for g in range(FG):
            pre = jnp.zeros((PIX, C), F32)
            for dy in range(3):
                for dx in range(3):
                    pre += dot(held[dx, g, 16 * dy : 16 * dy + PIX, :], k_ref[layer * 9 + dy * 3 + dx])
            value, slope = gelu_parts(pre)
            slope = jnp.where(keep, slope, 0.0).astype(BF)
            if layer == 0:
                g0_ref[g] = slope
                hold(held, g, jnp.where(keep, value, 0.0))
                a1_ref[:, g * C : (g + 1) * C] = held[1, g, 16 : 16 + C, :].T
            else:
                g1_ref[g] = slope


def forward(corners, pieces, offsets, kernels):
    slots = 16
    half = BOX // 2
    whole = lambda *shape: pl.BlockSpec(shape, lambda i, *_: (0,) * len(shape))
    columns = pl.BlockSpec((C, FG * C), lambda i, *_: (0, i))
    regions = pl.BlockSpec((FG, PIX, C), lambda i, *_: (i, 0, 0))
    return pl.pallas_call(
        forward_kernel,
        name="forward",
        out_shape=[
            jax.ShapeDtypeStruct((C, slots * C), BF),
            jax.ShapeDtypeStruct((C, slots * C), BF),
            jax.ShapeDtypeStruct((slots, PIX, C), BF),
            jax.ShapeDtypeStruct((slots, PIX, C), BF),
            jax.ShapeDtypeStruct((18, C, C), BF),
        ],
        grid_spec=pltpu.PrefetchScalarGridSpec(
            num_scalar_prefetch=1,
            grid=(slots // FG,),
            in_specs=[
                whole(BOX, BOX, C),
                whole(half, BOX, C),
                whole(half, BOX, C),
                whole(BOX, BOX, C),
                whole(half, BOX, C),
                whole(half, BOX, C),
                whole(32, 16),
                whole(18, C, C),
            ],
            out_specs=[columns, columns, regions, regions, whole(18, C, C)],
            scratch_shapes=[
                pltpu.VMEM((2 * BOX, 2 * BOX, C), BF),
                pltpu.VMEM((2, 16, WIN), F32),
                pltpu.VMEM((FG, 16, WIN), F32),
                pltpu.VMEM((FG, PIX, WIN), BF),
                pltpu.VMEM((3, FG, ROWS, C), BF),
            ],
        ),
        cost_estimate=pl.CostEstimate(
            flops=11_300_000_000, bytes_accessed=14 << 20, transcendentals=4_000_000
        ),
    )(corners, *pieces, offsets, kernels)


BG = 4


def top_grad(meta_ref, slot, in_ref, slope):
    live = slot < meta_ref[16]
    grad = in_ref[meta_ref[jnp.minimum(slot, 15)]].astype(F32) * slope.astype(F32)
    return jnp.where(live, grad, 0.0)


def add_tap(held, a_ref, acc, tap):
    dy, dx = divmod(tap, 3)
    grads = held[2 - dx, :, 32 - 16 * dy : 32 - 16 * dy + C, :].reshape(BG * C, C)
    acc[tap] += dot(a_ref[...], grads)


def input_grad(held, g, k_ref):
    total = jnp.zeros((PIX, C), F32)
    for dy in range(3):
        for dx in range(3):
            total += dot(
                held[2 - dx, g, 32 - 16 * dy : 32 - 16 * dy + PIX, :],
                k_ref[dy * 3 + dx],
            )
    return total.astype(BF)


def back_kernel(
    meta_ref, in_ref, first_ref, next_ref, g0_ref, k_ref, a1_ref, a0_ref,
    p_ref, o1_ref, o0_ref, upper, held, acc1, acc0,
):
    step = pl.program_id(0)
    now = step & 1

    @pl.when(step == 0)
    def _():
        clear_edges(upper.at[0], BG)
        clear_edges(upper.at[1], BG)
        clear_edges(held, BG)
        acc1[...] = jnp.zeros_like(acc1)
        acc0[...] = jnp.zeros_like(acc0)
        for g in range(BG):
            hold(upper.at[0], g, top_grad(meta_ref, g, in_ref, first_ref[g]))

    here = upper.at[now]
    later = upper.at[1 - now]

    def inner_grad(g, grad):
        grad = grad.astype(F32) * g0_ref[g].astype(F32)
        p_ref[g] = grad.astype(BF)
        hold(held, g, grad)

    grads = [input_grad(here, 0, k_ref)]
    for g in range(1, BG):
        grads.append(input_grad(here, g, k_ref))
        inner_grad(g - 1, grads[g - 1])
    for tap in range(9):
        add_tap(here, a1_ref, acc1, tap)
        if tap == 0:
            inner_grad(BG - 1, grads[BG - 1])
    for tap in range(9):
        add_tap(held, a0_ref, acc0, tap)
        if tap % 2 == 0 and tap // 2 < BG:
            g = tap // 2
            hold(later, g, top_grad(meta_ref, (step + 1) * BG + g, in_ref, next_ref[g]))

    @pl.when(step == pl.num_programs(0) - 1)
    def _():
        o1_ref[...] = acc1[...].astype(BF)
        o0_ref[...] = acc0[...].astype(BF)


def back(meta, incoming, slope1, slope0, kernels, acts1, acts0):
    slots = slope1.shape[0]
    steps = slots // BG
    whole = lambda *shape: pl.BlockSpec(shape, lambda i, *_: (0,) * len(shape))
    regions = pl.BlockSpec((BG, PIX, C), lambda i, *_: (i, 0, 0))
    columns = pl.BlockSpec((C, BG * C), lambda i, *_: (0, i))
    return pl.pallas_call(
        back_kernel,
        name="back",
        out_shape=[
            jax.ShapeDtypeStruct((slots, PIX, C), BF),
            jax.ShapeDtypeStruct((9, C, C), BF),
            jax.ShapeDtypeStruct((9, C, C), BF),
        ],
        grid_spec=pltpu.PrefetchScalarGridSpec(
            num_scalar_prefetch=1,
            grid=(steps,),
            in_specs=[
                whole(16, PIX, C),
                whole(BG, PIX, C),
                pl.BlockSpec((BG, PIX, C), lambda i, *_: (jnp.minimum(i + 1, steps - 1), 0, 0)),
                regions,
                pl.BlockSpec((9, C, C), lambda i, *_: (1, 0, 0)),
                columns,
                columns,
            ],
            out_specs=[regions, whole(9, C, C), whole(9, C, C)],
            scratch_shapes=[
                pltpu.VMEM((2, 3, BG, ROWS, C), BF),
                pltpu.VMEM((3, BG, ROWS, C), BF),
                pltpu.VMEM((9, C, C), F32),
                pltpu.VMEM((9, C, C), F32),
            ],
        ),
        cost_estimate=pl.CostEstimate(
            flops=14_000_000_000, bytes_accessed=16 << 20, transcendentals=0
        ),
    )(meta, incoming, slope1, slope1, slope0, kernels, acts1, acts0)


SG = 4
PART = 4


def spread_kernel(
    corner_ref, p_ref, off_ref, k_ref, tl_ref, tr_ref, bl_ref, br_ref, held, row_w, lanes, total
):
    step = pl.program_id(0)

    @pl.when(step == 0)
    def _():
        clear_edges(held, SG)
        total[...] = jnp.zeros_like(total)
        entry = lax.broadcasted_iota(jnp.int32, (32, C), 0)
        pixel = lax.broadcasted_iota(jnp.int32, (32, C), 1)
        for axis in range(2):
            index = pixel // PITCH if axis == 0 else 16 + (pixel & (PITCH - 1))
            pick = jnp.where(entry == index, 1.0, 0.0).astype(BF)
            lanes[axis] = dot(off_ref[...].astype(BF), pick)

    for g in range(SG):
        hold(held, g, p_ref[g].astype(F32))
    row_at = 4.0 * lax.broadcasted_iota(jnp.int32, (BOX, C), 0).astype(F32)
    col_at = 4.0 * lax.broadcasted_iota(jnp.int32, (SPAN, C), 0).astype(F32)
    grads = [
        jnp.concatenate([input_grad(held, g, k_ref), jnp.zeros((C - PIX, C), BF)], axis=0)
        for g in range(SG)
    ]
    for g in range(SG):
        slot = step * SG + g
        top = corner_ref[slot]
        left = pl.multiple_of(corner_ref[16 + slot] // 16 * 16, 16)
        row_w[g] = tent(row_at, lanes[0, pl.ds(slot, 1), :])
        col_w = tent(col_at, lanes[1, pl.ds(slot, 1), :])
        for at in range(0, BOX, PART):
            weight = jnp.concatenate(
                [(row_w[g, p : p + 1, :] * col_w).astype(BF) for p in range(at, at + PART)], axis=0
            )
            total[pl.ds(top + at, PART), pl.ds(left, SPAN), :] += dot(weight, grads[g]).reshape(
                PART, SPAN, C
            )

    @pl.when(step == pl.num_programs(0) - 1)
    def _():
        tl_ref[...] = total[0:BOX, 0:BOX, :]
        tr_ref[...] = total[0:BOX, BOX : 2 * BOX, :].astype(BF)
        bl_ref[...] = total[BOX : 2 * BOX, 0:BOX, :].astype(BF)
        br_ref[...] = total[BOX : 2 * BOX, BOX : 2 * BOX, :].astype(BF)


def spread(corners, inner, offsets, kernels):
    slots = inner.shape[0]
    whole = lambda *shape: pl.BlockSpec(shape, lambda i, *_: (0,) * len(shape))
    piece = lambda kind: jax.ShapeDtypeStruct((BOX, BOX, C), kind)
    return pl.pallas_call(
        spread_kernel,
        name="spread",
        out_shape=[piece(F32), piece(BF), piece(BF), piece(BF)],
        grid_spec=pltpu.PrefetchScalarGridSpec(
            num_scalar_prefetch=1,
            grid=(slots // SG,),
            in_specs=[
                pl.BlockSpec((SG, PIX, C), lambda i, *_: (i, 0, 0)),
                whole(16, 32),
                whole(9, C, C),
            ],
            out_specs=[whole(BOX, BOX, C)] * 4,
            scratch_shapes=[
                pltpu.VMEM((3, SG, ROWS, C), BF),
                pltpu.VMEM((SG, BOX, C), F32),
                pltpu.VMEM((2, 16, C), F32),
                pltpu.VMEM((2 * BOX, 2 * BOX, C), F32),
            ],
        ),
        cost_estimate=pl.CostEstimate(
            flops=7_000_000_000, bytes_accessed=6 << 20, transcendentals=0
        ),
    )(corners, inner, offsets, kernels)


def swap_cores(x):
    return lax.ppermute(x, "ha", [(i, i ^ 1) for i in range(lax.axis_size("ha"))])


def over_chips(pieces):
    down, across = lax.axis_size("ha"), lax.axis_size("wa")
    groups = [[h * across + w for h in range(c, down, 2) for w in range(across)] for c in range(2)]
    return lax.all_to_all(
        pieces, ("ha", "wa"), 0, 0, tiled=True, axis_index_groups=groups
    )


def pick_layer(index, first, second):
    return jnp.where(index == 0, first, second)


def local(features, counts, owner_perm, corners, offsets, kernels, cotangent):
    peers = lax.axis_size("wa")
    core = lax.axis_index("ha") % 2
    rows = BOX // 2
    cut = lambda x: (x[:rows], x[rows:])
    row_counts = lax.all_to_all(
        jnp.broadcast_to(counts[None], (peers, 1, 1)), "wa", 0, 0, tiled=True
    ).reshape(peers)
    from_right = [shifted(piece, "wa", -1) for piece in cut(features)]
    below = shifted(features, "ha", -1)
    outgoing, meta = route(row_counts, owner_perm, cotangent)
    corner = [shifted(piece, "ha", -1) for piece in from_right]
    incoming = lax.all_to_all(
        outgoing.reshape(peers, PIX, C), "wa", split_axis=0, concat_axis=0, tiled=True
    )
    pieces = (features, *from_right, below, *corner)
    places = jnp.concatenate(
        [offsets[:, :SIDE], offsets[:, SIDE:] + (corners[:, 1:2] % 16) * 4], axis=1
    ).astype(F32)
    pad = lambda x: jnp.pad(x, ((0, 0), (0, 2)), constant_values=-1000.0)
    places = jnp.concatenate([pad(places[:, :SIDE]), pad(places[:, SIDE:])], axis=1)
    place_cols = places.T
    corners = corners.T.reshape(-1)
    acts0, acts1, slope0, slope1, turned = forward(
        corners, pieces, place_cols, kernels.reshape(18, C, C)
    )
    inner, grad1, grad0 = back(meta, incoming, slope1, slope0, turned, acts1, acts0)
    mine = swap_cores(pick_layer(core, grad1, grad0)).astype(F32)
    mine = (mine + pick_layer(core, grad0, grad1).astype(F32)).astype(BF)
    chips = lax.axis_size("ha") // 2 * peers
    parts = over_chips(mine.reshape(chips, -1, C))
    tile, right, lower, corner = spread(corners, inner, places, turned)
    corner, lower = [shifted(piece, "ha", 1) for piece in (corner, lower)]
    side = shifted((right.astype(F32) + corner.astype(F32)).astype(BF), "wa", 1)
    tile = tile + lower.astype(F32)
    total = jnp.sum(parts.astype(F32), axis=0).astype(BF)
    whole = jnp.broadcast_to(total[None], (chips, *total.shape))
    mine = over_chips(whole).reshape(9, C, C)
    mine, tile, side = lax.optimization_barrier((mine, tile, side))
    tile = tile + side.astype(F32)
    other = swap_cores(mine)
    grads = jnp.stack([pick_layer(core, mine, other), pick_layer(core, other, mine)]).astype(F32)
    return (tile, grads.reshape(2, 3, 3, C, C))


def solution(mesh):
    in_specs = (
        P("ha", "wa", None),
        P("ha", "wa"),
        P("ha", None),
        P(("ha", "wa"), None),
        P(("ha", "wa"), None),
        P(),
        P(("ha", "wa"), None, None, None),
    )
    out_specs = (P("ha", "wa", None), P())

    return jax.shard_map(local, mesh=mesh, in_specs=in_specs, out_specs=out_specs, check_vma=False)
```

```python
import jax
import jax.numpy as jnp
from jax import lax
from jax.experimental import pallas as pl
from jax.experimental.pallas import tpu as pltpu
from jax.sharding import PartitionSpec as P

SIDE = 14
PITCH = 16
PIX = SIDE * PITCH
BOX = 32
SPAN = 48
WIN = BOX * SPAN
ROWS = 288
C = 256
BF = jnp.bfloat16
F32 = jnp.float32


def shifted(value, axis, steps):
    count = lax.axis_size(axis)
    first, last = (max(0, -steps), min(count, count - steps))
    return lax.ppermute(value, axis, [(source, source + steps) for source in range(first, last)])


def dot(a, b, dims=(((1,), (0,)), ((), ()))):
    return lax.dot_general(a, b, dims, preferred_element_type=F32)


def inside(rows):
    pixel = lax.broadcasted_iota(jnp.int32, (rows, C), 0)
    return (pixel & (PITCH - 1)) < SIDE


def clear_edges(held, copies):
    for shift in range(3):
        for g in range(copies):
            held[shift, g, 0:16, :] = jnp.zeros((16, C), BF)
            held[shift, g, 16 + PIX : ROWS, :] = jnp.zeros((ROWS - 16 - PIX, C), BF)


def hold(held, g, value):
    held[0, g, 16 : 16 + PIX, :] = pltpu.roll(value, 1, 0).astype(BF)
    held[1, g, 16 : 16 + PIX, :] = value.astype(BF)
    held[2, g, 16 : 16 + PIX, :] = pltpu.roll(value, PIX - 1, 0).astype(BF)


def tent(places, offsets):
    return jnp.maximum(0.0, 1.0 - jnp.abs(places - offsets) * 0.25)


def gelu_parts(v):
    cdf = 0.5 * (1.0 + lax.erf(v * 0.7071067811865476))
    slope = cdf + v * (jnp.exp(v * v * -0.5) * 0.3989422804014327)
    return v * cdf, slope


def route_kernel(count_ref, perm_ref, x_ref, o_ref, meta_ref):
    peers = o_ref.shape[0]
    here = lax.axis_index("wa")
    position = jnp.int32(0)
    for i in range(peers):
        position = jnp.where(perm_ref[0, i] == here, i, position)
    start = jnp.int32(0)
    here_start = jnp.int32(0)
    gap = jnp.zeros((SIDE, PITCH - SIDE, C), BF)
    for i in range(peers):
        here_start = jnp.where(here == i, start, here_start)
        arrival = start + ((position - start) & (peers - 1))
        region = jnp.clip(arrival // peers, 0, x_ref.shape[0] - 1)
        o_ref[i, :, 0:SIDE, :] = x_ref[region]
        o_ref[i, :, SIDE:PITCH, :] = gap
        start = start + count_ref[i]
    for i in range(peers):
        meta_ref[i] = perm_ref[0, (here_start + i) & (peers - 1)]
    meta_ref[peers] = count_ref[here]


def route(counts, perm, cotangent):
    peers = counts.shape[0]
    smem = pl.BlockSpec(memory_space=pltpu.SMEM)
    vmem = pl.BlockSpec(memory_space=pltpu.VMEM)
    return pl.pallas_call(
        route_kernel,
        name="route",
        out_shape=[
            jax.ShapeDtypeStruct((peers, SIDE, PITCH, C), BF),
            jax.ShapeDtypeStruct((peers + 1,), jnp.int32),
        ],
        in_specs=[smem, smem, vmem],
        out_specs=[vmem, smem],
        cost_estimate=pl.CostEstimate(flops=0, bytes_accessed=4 << 20, transcendentals=0),
    )(counts, perm, cotangent)


FG = 4


def forward_kernel(
    corner_ref, tl_ref, tr_ref, bl_ref, br_ref, off_ref, k_ref,
    a0_ref, a1_ref, g0_ref, g1_ref, t_ref, ext, places, row_w, weight, held,
):
    step = pl.program_id(0)

    @pl.when(step == 0)
    def _():
        clear_edges(held, FG)
        ext[0:BOX, 0:BOX, :] = tl_ref[...]
        ext[0:BOX, BOX : 2 * BOX, :] = tr_ref[...]
        ext[BOX : 2 * BOX, 0:BOX, :] = bl_ref[...]
        ext[BOX : 2 * BOX, BOX : 2 * BOX, :] = br_ref[...]
        at = lax.broadcasted_iota(jnp.int32, (16, WIN), 1).astype(F32)
        row = jnp.floor((at + 0.5) * (1.0 / SPAN))
        places[0] = 4.0 * row
        places[1] = 4.0 * (at - SPAN * row)

    keep = inside(PIX)
    lane = lax.broadcasted_iota(jnp.int32, (32, 16), 1)
    for g in range(FG):
        slot = step * FG + g
        top = corner_ref[slot]
        left = pl.multiple_of(corner_ref[16 + slot] // 16 * 16, 16)
        offsets = jnp.sum(jnp.where(lane == slot, off_ref[...], 0.0), axis=1, keepdims=True)
        row_w[g] = tent(places[0], offsets[0:16])
        col_w = tent(places[1], offsets[16:32])
        for i in range(SIDE):
            weight[g, i * PITCH : (i + 1) * PITCH, :] = (row_w[g, i : i + 1, :] * col_w).astype(BF)
        window = ext[pl.ds(top, BOX), pl.ds(left, SPAN), :].reshape(WIN, C)
        hold(held, g, dot(weight[g], window))
        a0_ref[:, g * C : (g + 1) * C] = held[1, g, 16 : 16 + C, :].T
    for i in range(5):
        tap = jnp.minimum(step * 5 + i, 17)
        t_ref[tap] = k_ref[tap].T
    for layer in range(2):
        for g in range(FG):
            pre = jnp.zeros((PIX, C), F32)
            for dy in range(3):
                for dx in range(3):
                    pre += dot(held[dx, g, 16 * dy : 16 * dy + PIX, :], k_ref[layer * 9 + dy * 3 + dx])
            value, slope = gelu_parts(pre)
            slope = jnp.where(keep, slope, 0.0).astype(BF)
            if layer == 0:
                g0_ref[g] = slope
                hold(held, g, jnp.where(keep, value, 0.0))
                a1_ref[:, g * C : (g + 1) * C] = held[1, g, 16 : 16 + C, :].T
            else:
                g1_ref[g] = slope


def forward(corners, pieces, offsets, kernels):
    slots = 16
    whole = lambda *shape: pl.BlockSpec(shape, lambda i, *_: (0,) * len(shape))
    columns = pl.BlockSpec((C, FG * C), lambda i, *_: (0, i))
    regions = pl.BlockSpec((FG, PIX, C), lambda i, *_: (i, 0, 0))
    return pl.pallas_call(
        forward_kernel,
        name="forward",
        out_shape=[
            jax.ShapeDtypeStruct((C, slots * C), BF),
            jax.ShapeDtypeStruct((C, slots * C), BF),
            jax.ShapeDtypeStruct((slots, PIX, C), BF),
            jax.ShapeDtypeStruct((slots, PIX, C), BF),
            jax.ShapeDtypeStruct((18, C, C), BF),
        ],
        grid_spec=pltpu.PrefetchScalarGridSpec(
            num_scalar_prefetch=1,
            grid=(slots // FG,),
            in_specs=[
                whole(BOX, BOX, C),
                whole(BOX, BOX, C),
                whole(BOX, BOX, C),
                whole(BOX, BOX, C),
                whole(32, 16),
                whole(18, C, C),
            ],
            out_specs=[columns, columns, regions, regions, whole(18, C, C)],
            scratch_shapes=[
                pltpu.VMEM((2 * BOX, 2 * BOX, C), BF),
                pltpu.VMEM((2, 16, WIN), F32),
                pltpu.VMEM((FG, 16, WIN), F32),
                pltpu.VMEM((FG, PIX, WIN), BF),
                pltpu.VMEM((3, FG, ROWS, C), BF),
            ],
        ),
        cost_estimate=pl.CostEstimate(
            flops=11_300_000_000, bytes_accessed=14 << 20, transcendentals=4_000_000
        ),
    )(corners, *pieces, offsets, kernels)


BG = 4


def top_grad(meta_ref, slot, in_ref, slope):
    live = slot < meta_ref[16]
    grad = in_ref[meta_ref[jnp.minimum(slot, 15)]].astype(F32) * slope.astype(F32)
    return jnp.where(live, grad, 0.0)


def add_tap(held, a_ref, acc, tap):
    dy, dx = divmod(tap, 3)
    grads = held[2 - dx, :, 32 - 16 * dy : 32 - 16 * dy + C, :].reshape(BG * C, C)
    acc[tap] += dot(a_ref[...], grads)


def input_grad(held, g, k_ref):
    total = jnp.zeros((PIX, C), F32)
    for dy in range(3):
        for dx in range(3):
            total += dot(
                held[2 - dx, g, 32 - 16 * dy : 32 - 16 * dy + PIX, :],
                k_ref[dy * 3 + dx],
            )
    return total.astype(BF)


def back_kernel(
    meta_ref, in_ref, first_ref, next_ref, g0_ref, k_ref, a1_ref, a0_ref,
    p_ref, keep_ref, send_ref, upper, held, acc1, acc0,
):
    step = pl.program_id(0)
    now = step & 1

    @pl.when(step == 0)
    def _():
        clear_edges(upper.at[0], BG)
        clear_edges(upper.at[1], BG)
        clear_edges(held, BG)
        acc1[...] = jnp.zeros_like(acc1)
        acc0[...] = jnp.zeros_like(acc0)
        for g in range(BG):
            hold(upper.at[0], g, top_grad(meta_ref, g, in_ref, first_ref[g]))

    here = upper.at[now]
    later = upper.at[1 - now]

    def inner_grad(g, grad):
        grad = grad.astype(F32) * g0_ref[g].astype(F32)
        p_ref[g] = grad.astype(BF)
        hold(held, g, grad)

    grads = [input_grad(here, 0, k_ref)]
    for g in range(1, BG):
        grads.append(input_grad(here, g, k_ref))
        inner_grad(g - 1, grads[g - 1])
    for tap in range(9):
        add_tap(here, a1_ref, acc1, tap)
        if tap == 0:
            inner_grad(BG - 1, grads[BG - 1])
    for tap in range(9):
        add_tap(held, a0_ref, acc0, tap)
        if tap % 2 == 0 and tap // 2 < BG:
            g = tap // 2
            hold(later, g, top_grad(meta_ref, (step + 1) * BG + g, in_ref, next_ref[g]))

    @pl.when(step == pl.num_programs(0) - 1)
    def _():
        keeps_first = (lax.axis_index("ha") & 1) == 0

        @pl.when(keeps_first)
        def _():
            keep_ref[...] = acc0[...].astype(BF)
            send_ref[...] = acc1[...].astype(BF)

        @pl.when(jnp.logical_not(keeps_first))
        def _():
            keep_ref[...] = acc1[...].astype(BF)
            send_ref[...] = acc0[...].astype(BF)


def back(meta, incoming, slope1, slope0, kernels, acts1, acts0):
    slots = slope1.shape[0]
    steps = slots // BG
    whole = lambda *shape: pl.BlockSpec(shape, lambda i, *_: (0,) * len(shape))
    regions = pl.BlockSpec((BG, PIX, C), lambda i, *_: (i, 0, 0))
    columns = pl.BlockSpec((C, BG * C), lambda i, *_: (0, i))
    return pl.pallas_call(
        back_kernel,
        name="back",
        out_shape=[
            jax.ShapeDtypeStruct((slots, PIX, C), BF),
            jax.ShapeDtypeStruct((9, C, C), BF),
            jax.ShapeDtypeStruct((9, C, C), BF),
        ],
        grid_spec=pltpu.PrefetchScalarGridSpec(
            num_scalar_prefetch=1,
            grid=(steps,),
            in_specs=[
                whole(16, PIX, C),
                whole(BG, PIX, C),
                pl.BlockSpec((BG, PIX, C), lambda i, *_: (jnp.minimum(i + 1, steps - 1), 0, 0)),
                regions,
                pl.BlockSpec((9, C, C), lambda i, *_: (1, 0, 0)),
                columns,
                columns,
            ],
            out_specs=[regions, whole(9, C, C), whole(9, C, C)],
            scratch_shapes=[
                pltpu.VMEM((2, 3, BG, ROWS, C), BF),
                pltpu.VMEM((3, BG, ROWS, C), BF),
                pltpu.VMEM((9, C, C), F32),
                pltpu.VMEM((9, C, C), F32),
            ],
        ),
        cost_estimate=pl.CostEstimate(
            flops=14_000_000_000, bytes_accessed=16 << 20, transcendentals=0
        ),
    )(meta, incoming, slope1, slope1, slope0, kernels, acts1, acts0)


SG = 4
PART = 4


def spread_kernel(
    corner_ref, p_ref, off_ref, k_ref, tl_ref, tr_ref, bl_ref, br_ref, held, row_w, lanes, total
):
    step = pl.program_id(0)

    @pl.when(step == 0)
    def _():
        clear_edges(held, SG)
        total[...] = jnp.zeros_like(total)
        entry = lax.broadcasted_iota(jnp.int32, (32, C), 0)
        pixel = lax.broadcasted_iota(jnp.int32, (32, C), 1)
        for axis in range(2):
            index = pixel // PITCH if axis == 0 else 16 + (pixel & (PITCH - 1))
            pick = jnp.where(entry == index, 1.0, 0.0).astype(BF)
            lanes[axis] = dot(off_ref[...].astype(BF), pick)

    for g in range(SG):
        hold(held, g, p_ref[g].astype(F32))
    row_at = 4.0 * lax.broadcasted_iota(jnp.int32, (BOX, C), 0).astype(F32)
    col_at = 4.0 * lax.broadcasted_iota(jnp.int32, (SPAN, C), 0).astype(F32)
    grads = [
        jnp.concatenate([input_grad(held, g, k_ref), jnp.zeros((C - PIX, C), BF)], axis=0)
        for g in range(SG)
    ]
    for g in range(SG):
        slot = step * SG + g
        top = corner_ref[slot]
        left = pl.multiple_of(corner_ref[16 + slot] // 16 * 16, 16)
        row_w[g] = tent(row_at, lanes[0, pl.ds(slot, 1), :])
        col_w = tent(col_at, lanes[1, pl.ds(slot, 1), :])
        for at in range(0, BOX, PART):
            weight = jnp.concatenate(
                [(row_w[g, p : p + 1, :] * col_w).astype(BF) for p in range(at, at + PART)], axis=0
            )
            total[pl.ds(top + at, PART), pl.ds(left, SPAN), :] += dot(weight, grads[g]).reshape(
                PART, SPAN, C
            )

    @pl.when(step == pl.num_programs(0) - 1)
    def _():
        tl_ref[...] = total[0:BOX, 0:BOX, :]
        tr_ref[...] = total[0:BOX, BOX : 2 * BOX, :].astype(BF)
        bl_ref[...] = total[BOX : 2 * BOX, 0:BOX, :].astype(BF)
        br_ref[...] = total[BOX : 2 * BOX, BOX : 2 * BOX, :].astype(BF)


def spread(corners, inner, offsets, kernels):
    slots = inner.shape[0]
    whole = lambda *shape: pl.BlockSpec(shape, lambda i, *_: (0,) * len(shape))
    piece = lambda kind: jax.ShapeDtypeStruct((BOX, BOX, C), kind)
    return pl.pallas_call(
        spread_kernel,
        name="spread",
        out_shape=[piece(F32), piece(BF), piece(BF), piece(BF)],
        grid_spec=pltpu.PrefetchScalarGridSpec(
            num_scalar_prefetch=1,
            grid=(slots // SG,),
            in_specs=[
                pl.BlockSpec((SG, PIX, C), lambda i, *_: (i, 0, 0)),
                whole(16, 32),
                whole(9, C, C),
            ],
            out_specs=[whole(BOX, BOX, C)] * 4,
            scratch_shapes=[
                pltpu.VMEM((3, SG, ROWS, C), BF),
                pltpu.VMEM((SG, BOX, C), F32),
                pltpu.VMEM((2, 16, C), F32),
                pltpu.VMEM((2 * BOX, 2 * BOX, C), F32),
            ],
        ),
        cost_estimate=pl.CostEstimate(
            flops=7_000_000_000, bytes_accessed=6 << 20, transcendentals=0
        ),
    )(corners, inner, offsets, kernels)


def swap_cores(x):
    return lax.ppermute(x, "ha", [(i, i ^ 1) for i in range(lax.axis_size("ha"))])


def pick_layer(index, first, second):
    return jnp.where(index == 0, first, second)


def local(features, counts, owner_perm, corners, offsets, kernels, cotangent):
    peers = lax.axis_size("wa")
    core = lax.axis_index("ha") % 2
    row_counts = lax.all_to_all(
        jnp.broadcast_to(counts[None], (peers, 1, 1)), "wa", 0, 0, tiled=True
    ).reshape(peers)
    from_right = shifted(features, "wa", -1)
    below = shifted(features, "ha", -1)
    outgoing, meta = route(row_counts, owner_perm, cotangent)
    corner = shifted(from_right, "ha", -1)
    incoming = lax.all_to_all(
        outgoing.reshape(peers, PIX, C), "wa", split_axis=0, concat_axis=0, tiled=True
    )
    pieces = (features, from_right, below, corner)
    places = jnp.concatenate(
        [offsets[:, :SIDE], offsets[:, SIDE:] + (corners[:, 1:2] % 16) * 4], axis=1
    ).astype(F32)
    pad = lambda x: jnp.pad(x, ((0, 0), (0, 2)), constant_values=-1000.0)
    places = jnp.concatenate([pad(places[:, :SIDE]), pad(places[:, SIDE:])], axis=1)
    place_cols = places.T
    corners = corners.T.reshape(-1)
    acts0, acts1, slope0, slope1, turned = forward(
        corners, pieces, place_cols, kernels.reshape(18, C, C)
    )
    inner, keep, send = back(meta, incoming, slope1, slope0, turned, acts1, acts0)
    mine = (keep.astype(F32) + swap_cores(send).astype(F32)).astype(BF)
    parts = lax.all_to_all(mine.reshape(peers, -1, C), "wa", 0, 0, tiled=True)
    tile, right, lower, corner = spread(corners, inner, places, turned)
    corner, lower = [shifted(piece, "ha", 1) for piece in (corner, lower)]
    part = jnp.sum(parts.astype(F32), axis=0).astype(BF)
    count = lax.axis_size("ha")
    total = part.astype(F32)
    for hop in range(2, count, 2):
        moved = lax.ppermute(part, "ha", [(i, (i + hop) % count) for i in range(count)])
        total = total + moved.astype(F32)
    whole = jnp.broadcast_to(total.astype(BF)[None], (peers, *total.shape))
    mine = lax.all_to_all(whole, "wa", 0, 0, tiled=True).reshape(9, C, C)
    side = shifted((right.astype(F32) + corner.astype(F32)).astype(BF), "wa", 1)
    tile = tile + lower.astype(F32)
    mine, tile, side = lax.optimization_barrier((mine, tile, side))
    tile = tile + side.astype(F32)
    other = swap_cores(mine)
    grads = jnp.stack([pick_layer(core, mine, other), pick_layer(core, other, mine)]).astype(F32)
    return (tile, grads.reshape(2, 3, 3, C, C))


def solution(mesh):
    in_specs = (
        P("ha", "wa", None),
        P("ha", "wa"),
        P("ha", None),
        P(("ha", "wa"), None),
        P(("ha", "wa"), None),
        P(),
        P(("ha", "wa"), None, None, None),
    )
    out_specs = (P("ha", "wa", None), P())

    return jax.shard_map(local, mesh=mesh, in_specs=in_specs, out_specs=out_specs, check_vma=False)
```

```python
import jax
import jax.numpy as jnp
from jax import lax
from jax.experimental import pallas as pl
from jax.experimental.pallas import tpu as pltpu
from jax.sharding import PartitionSpec as P

SIDE = 14
PITCH = 16
PIX = SIDE * PITCH
BOX = 32
SPAN = 48
WIN = BOX * SPAN
ROWS = 288
C = 256
BF = jnp.bfloat16
F32 = jnp.float32


def shifted(value, axis, steps):
    count = lax.axis_size(axis)
    first, last = (max(0, -steps), min(count, count - steps))
    return lax.ppermute(value, axis, [(source, source + steps) for source in range(first, last)])


def dot(a, b, dims=(((1,), (0,)), ((), ()))):
    return lax.dot_general(a, b, dims, preferred_element_type=F32)


def inside(rows):
    pixel = lax.broadcasted_iota(jnp.int32, (rows, C), 0)
    return (pixel & (PITCH - 1)) < SIDE


def clear_edges(held, copies):
    for shift in range(3):
        for g in range(copies):
            held[shift, g, 0:16, :] = jnp.zeros((16, C), BF)
            held[shift, g, 16 + PIX : ROWS, :] = jnp.zeros((ROWS - 16 - PIX, C), BF)


def hold(held, g, value):
    held[0, g, 16 : 16 + PIX, :] = pltpu.roll(value, 1, 0).astype(BF)
    held[1, g, 16 : 16 + PIX, :] = value.astype(BF)
    held[2, g, 16 : 16 + PIX, :] = pltpu.roll(value, PIX - 1, 0).astype(BF)


def tent(places, offsets):
    return jnp.maximum(0.0, 1.0 - jnp.abs(places - offsets) * 0.25)


def gelu_parts(v):
    cdf = 0.5 * (1.0 + lax.erf(v * 0.7071067811865476))
    slope = cdf + v * (jnp.exp(v * v * -0.5) * 0.3989422804014327)
    return v * cdf, slope


def route_kernel(count_ref, perm_ref, x_ref, o_ref, meta_ref):
    peers = o_ref.shape[0]
    here = lax.axis_index("wa")
    position = jnp.int32(0)
    for i in range(peers):
        position = jnp.where(perm_ref[0, i] == here, i, position)
    start = jnp.int32(0)
    here_start = jnp.int32(0)
    gap = jnp.zeros((SIDE, PITCH - SIDE, C), BF)
    for i in range(peers):
        here_start = jnp.where(here == i, start, here_start)
        arrival = start + ((position - start) & (peers - 1))
        region = jnp.clip(arrival // peers, 0, x_ref.shape[0] - 1)
        o_ref[i, :, 0:SIDE, :] = x_ref[region]
        o_ref[i, :, SIDE:PITCH, :] = gap
        start = start + count_ref[i]
    for i in range(peers):
        meta_ref[i] = perm_ref[0, (here_start + i) & (peers - 1)]
    meta_ref[peers] = count_ref[here]


def route(counts, perm, cotangent):
    peers = counts.shape[0]
    smem = pl.BlockSpec(memory_space=pltpu.SMEM)
    vmem = pl.BlockSpec(memory_space=pltpu.VMEM)
    return pl.pallas_call(
        route_kernel,
        name="route",
        out_shape=[
            jax.ShapeDtypeStruct((peers, SIDE, PITCH, C), BF),
            jax.ShapeDtypeStruct((peers + 1,), jnp.int32),
        ],
        in_specs=[smem, smem, vmem],
        out_specs=[vmem, smem],
        cost_estimate=pl.CostEstimate(flops=0, bytes_accessed=4 << 20, transcendentals=0),
    )(counts, perm, cotangent)


FG = 4


def forward_kernel(
    corner_ref, tl_ref, tr_ref, bl_ref, br_ref, off_ref, k_ref,
    a0_ref, a1_ref, g0_ref, g1_ref, t_ref, ext, places, row_w, weight, held,
):
    step = pl.program_id(0)

    @pl.when(step == 0)
    def _():
        clear_edges(held, FG)
        ext[0:BOX, 0:BOX, :] = tl_ref[...]
        ext[0:BOX, BOX : 2 * BOX, :] = tr_ref[...]
        ext[BOX : 2 * BOX, 0:BOX, :] = bl_ref[...]
        ext[BOX : 2 * BOX, BOX : 2 * BOX, :] = br_ref[...]
        at = lax.broadcasted_iota(jnp.int32, (16, WIN), 1).astype(F32)
        row = jnp.floor((at + 0.5) * (1.0 / SPAN))
        places[0] = 4.0 * row
        places[1] = 4.0 * (at - SPAN * row)

    keep = inside(PIX)
    lane = lax.broadcasted_iota(jnp.int32, (32, 16), 1)
    for g in range(FG):
        slot = step * FG + g
        top = corner_ref[slot]
        left = pl.multiple_of(corner_ref[16 + slot] // 16 * 16, 16)
        offsets = jnp.sum(jnp.where(lane == slot, off_ref[...], 0.0), axis=1, keepdims=True)
        row_w[g] = tent(places[0], offsets[0:16])
        col_w = tent(places[1], offsets[16:32])
        for i in range(SIDE):
            weight[g, i * PITCH : (i + 1) * PITCH, :] = (row_w[g, i : i + 1, :] * col_w).astype(BF)
        window = ext[pl.ds(top, BOX), pl.ds(left, SPAN), :].reshape(WIN, C)
        hold(held, g, dot(weight[g], window))
        a0_ref[:, g * C : (g + 1) * C] = held[1, g, 16 : 16 + C, :].T
    for i in range(5):
        tap = jnp.minimum(step * 5 + i, 17)
        t_ref[tap] = k_ref[tap].T
    for layer in range(2):
        for g in range(FG):
            pre = jnp.zeros((PIX, C), F32)
            for dy in range(3):
                for dx in range(3):
                    pre += dot(held[dx, g, 16 * dy : 16 * dy + PIX, :], k_ref[layer * 9 + dy * 3 + dx])
            value, slope = gelu_parts(pre)
            slope = jnp.where(keep, slope, 0.0).astype(BF)
            if layer == 0:
                g0_ref[g] = slope
                hold(held, g, jnp.where(keep, value, 0.0))
                a1_ref[:, g * C : (g + 1) * C] = held[1, g, 16 : 16 + C, :].T
            else:
                g1_ref[g] = slope


def forward(corners, pieces, offsets, kernels):
    slots = 16
    whole = lambda *shape: pl.BlockSpec(shape, lambda i, *_: (0,) * len(shape))
    columns = pl.BlockSpec((C, FG * C), lambda i, *_: (0, i))
    regions = pl.BlockSpec((FG, PIX, C), lambda i, *_: (i, 0, 0))
    return pl.pallas_call(
        forward_kernel,
        name="forward",
        out_shape=[
            jax.ShapeDtypeStruct((C, slots * C), BF),
            jax.ShapeDtypeStruct((C, slots * C), BF),
            jax.ShapeDtypeStruct((slots, PIX, C), BF),
            jax.ShapeDtypeStruct((slots, PIX, C), BF),
            jax.ShapeDtypeStruct((18, C, C), BF),
        ],
        grid_spec=pltpu.PrefetchScalarGridSpec(
            num_scalar_prefetch=1,
            grid=(slots // FG,),
            in_specs=[
                whole(BOX, BOX, C),
                pl.BlockSpec(memory_space=pltpu.VMEM),
                pl.BlockSpec(memory_space=pltpu.VMEM),
                pl.BlockSpec(memory_space=pltpu.VMEM),
                whole(32, 16),
                whole(18, C, C),
            ],
            out_specs=[columns, columns, regions, regions, whole(18, C, C)],
            scratch_shapes=[
                pltpu.VMEM((2 * BOX, 2 * BOX, C), BF),
                pltpu.VMEM((2, 16, WIN), F32),
                pltpu.VMEM((FG, 16, WIN), F32),
                pltpu.VMEM((FG, PIX, WIN), BF),
                pltpu.VMEM((3, FG, ROWS, C), BF),
            ],
        ),
        cost_estimate=pl.CostEstimate(
            flops=11_300_000_000, bytes_accessed=14 << 20, transcendentals=4_000_000
        ),
    )(corners, *pieces, offsets, kernels)


BG = 4


def top_grad(meta_ref, slot, in_ref, slope):
    live = slot < meta_ref[16]
    grad = in_ref[meta_ref[jnp.minimum(slot, 15)]].astype(F32) * slope.astype(F32)
    return jnp.where(live, grad, 0.0)


def add_tap(held, a_ref, acc, tap):
    dy, dx = divmod(tap, 3)
    grads = held[2 - dx, :, 32 - 16 * dy : 32 - 16 * dy + C, :].reshape(BG * C, C)
    acc[tap] += dot(a_ref[...], grads)


def input_grad(held, g, k_ref):
    total = jnp.zeros((PIX, C), F32)
    for dy in range(3):
        for dx in range(3):
            total += dot(
                held[2 - dx, g, 32 - 16 * dy : 32 - 16 * dy + PIX, :],
                k_ref[dy * 3 + dx],
            )
    return total.astype(BF)


def back_kernel(
    meta_ref, in_ref, first_ref, next_ref, g0_ref, k_ref, a1_ref, a0_ref,
    p_ref, keep_ref, send_ref, upper, held, acc1, acc0,
):
    step = pl.program_id(0)
    now = step & 1

    @pl.when(step == 0)
    def _():
        clear_edges(upper.at[0], BG)
        clear_edges(upper.at[1], BG)
        clear_edges(held, BG)
        acc1[...] = jnp.zeros_like(acc1)
        acc0[...] = jnp.zeros_like(acc0)
        for g in range(BG):
            hold(upper.at[0], g, top_grad(meta_ref, g, in_ref, first_ref[g]))

    here = upper.at[now]
    later = upper.at[1 - now]

    def inner_grad(g, grad):
        grad = grad.astype(F32) * g0_ref[g].astype(F32)
        p_ref[g] = grad.astype(BF)
        hold(held, g, grad)

    grads = [input_grad(here, 0, k_ref)]
    for g in range(1, BG):
        grads.append(input_grad(here, g, k_ref))
        inner_grad(g - 1, grads[g - 1])
    for tap in range(9):
        add_tap(here, a1_ref, acc1, tap)
        if tap == 0:
            inner_grad(BG - 1, grads[BG - 1])
    for tap in range(9):
        add_tap(held, a0_ref, acc0, tap)
        if tap % 2 == 0 and tap // 2 < BG:
            g = tap // 2
            hold(later, g, top_grad(meta_ref, (step + 1) * BG + g, in_ref, next_ref[g]))

    @pl.when(step == pl.num_programs(0) - 1)
    def _():
        keeps_first = (lax.axis_index("ha") & 1) == 0

        @pl.when(keeps_first)
        def _():
            keep_ref[...] = acc0[...].astype(BF)
            send_ref[...] = acc1[...].astype(BF)

        @pl.when(jnp.logical_not(keeps_first))
        def _():
            keep_ref[...] = acc1[...].astype(BF)
            send_ref[...] = acc0[...].astype(BF)


def back(meta, incoming, slope1, slope0, kernels, acts1, acts0):
    slots = slope1.shape[0]
    steps = slots // BG
    whole = lambda *shape: pl.BlockSpec(shape, lambda i, *_: (0,) * len(shape))
    regions = pl.BlockSpec((BG, PIX, C), lambda i, *_: (i, 0, 0))
    columns = pl.BlockSpec((C, BG * C), lambda i, *_: (0, i))
    return pl.pallas_call(
        back_kernel,
        name="back",
        out_shape=[
            jax.ShapeDtypeStruct((slots, PIX, C), BF),
            jax.ShapeDtypeStruct((9, C, C), BF),
            jax.ShapeDtypeStruct((9, C, C), BF),
        ],
        grid_spec=pltpu.PrefetchScalarGridSpec(
            num_scalar_prefetch=1,
            grid=(steps,),
            in_specs=[
                pl.BlockSpec(memory_space=pltpu.VMEM),
                whole(BG, PIX, C),
                pl.BlockSpec((BG, PIX, C), lambda i, *_: (jnp.minimum(i + 1, steps - 1), 0, 0)),
                regions,
                pl.BlockSpec((9, C, C), lambda i, *_: (1, 0, 0)),
                columns,
                columns,
            ],
            out_specs=[regions, whole(9, C, C), whole(9, C, C)],
            scratch_shapes=[
                pltpu.VMEM((2, 3, BG, ROWS, C), BF),
                pltpu.VMEM((3, BG, ROWS, C), BF),
                pltpu.VMEM((9, C, C), F32),
                pltpu.VMEM((9, C, C), F32),
            ],
        ),
        cost_estimate=pl.CostEstimate(
            flops=14_000_000_000, bytes_accessed=16 << 20, transcendentals=0
        ),
    )(meta, incoming, slope1, slope1, slope0, kernels, acts1, acts0)


SG = 4
PART = 4


def spread_kernel(
    corner_ref, p_ref, off_ref, k_ref, tl_ref, tr_ref, bl_ref, br_ref, held, row_w, lanes, total
):
    step = pl.program_id(0)

    @pl.when(step == 0)
    def _():
        clear_edges(held, SG)
        total[...] = jnp.zeros_like(total)
        entry = lax.broadcasted_iota(jnp.int32, (32, C), 0)
        pixel = lax.broadcasted_iota(jnp.int32, (32, C), 1)
        for axis in range(2):
            index = pixel // PITCH if axis == 0 else 16 + (pixel & (PITCH - 1))
            pick = jnp.where(entry == index, 1.0, 0.0).astype(BF)
            lanes[axis] = dot(off_ref[...].astype(BF), pick)

    for g in range(SG):
        hold(held, g, p_ref[g].astype(F32))
    row_at = 4.0 * lax.broadcasted_iota(jnp.int32, (BOX, C), 0).astype(F32)
    col_at = 4.0 * lax.broadcasted_iota(jnp.int32, (SPAN, C), 0).astype(F32)
    grads = [
        jnp.concatenate([input_grad(held, g, k_ref), jnp.zeros((C - PIX, C), BF)], axis=0)
        for g in range(SG)
    ]
    for g in range(SG):
        slot = step * SG + g
        top = corner_ref[slot]
        left = pl.multiple_of(corner_ref[16 + slot] // 16 * 16, 16)
        row_w[g] = tent(row_at, lanes[0, pl.ds(slot, 1), :])
        col_w = tent(col_at, lanes[1, pl.ds(slot, 1), :])
        for at in range(0, BOX, PART):
            weight = jnp.concatenate(
                [(row_w[g, p : p + 1, :] * col_w).astype(BF) for p in range(at, at + PART)], axis=0
            )
            total[pl.ds(top + at, PART), pl.ds(left, SPAN), :] += dot(weight, grads[g]).reshape(
                PART, SPAN, C
            )

    @pl.when(step == pl.num_programs(0) - 1)
    def _():
        tl_ref[...] = total[0:BOX, 0:BOX, :]
        tr_ref[...] = total[0:BOX, BOX : 2 * BOX, :].astype(BF)
        bl_ref[...] = total[BOX : 2 * BOX, 0:BOX, :].astype(BF)
        br_ref[...] = total[BOX : 2 * BOX, BOX : 2 * BOX, :].astype(BF)


def spread(corners, inner, offsets, kernels):
    slots = inner.shape[0]
    whole = lambda *shape: pl.BlockSpec(shape, lambda i, *_: (0,) * len(shape))
    piece = lambda kind: jax.ShapeDtypeStruct((BOX, BOX, C), kind)
    return pl.pallas_call(
        spread_kernel,
        name="spread",
        out_shape=[piece(F32), piece(BF), piece(BF), piece(BF)],
        grid_spec=pltpu.PrefetchScalarGridSpec(
            num_scalar_prefetch=1,
            grid=(slots // SG,),
            in_specs=[
                pl.BlockSpec((SG, PIX, C), lambda i, *_: (i, 0, 0)),
                whole(16, 32),
                whole(9, C, C),
            ],
            out_specs=[whole(BOX, BOX, C)] * 4,
            scratch_shapes=[
                pltpu.VMEM((3, SG, ROWS, C), BF),
                pltpu.VMEM((SG, BOX, C), F32),
                pltpu.VMEM((2, 16, C), F32),
                pltpu.VMEM((2 * BOX, 2 * BOX, C), F32),
            ],
        ),
        cost_estimate=pl.CostEstimate(
            flops=7_000_000_000, bytes_accessed=6 << 20, transcendentals=0
        ),
    )(corners, inner, offsets, kernels)


def swap_cores(x):
    return lax.ppermute(x, "ha", [(i, i ^ 1) for i in range(lax.axis_size("ha"))])


def pick_layer(index, first, second):
    return jnp.where(index == 0, first, second)


def local(features, counts, owner_perm, corners, offsets, kernels, cotangent):
    peers = lax.axis_size("wa")
    core = lax.axis_index("ha") % 2
    row_counts = lax.all_to_all(
        jnp.broadcast_to(counts[None], (peers, 1, 1)), "wa", 0, 0, tiled=True
    ).reshape(peers)
    from_right = shifted(features, "wa", -1)
    below = shifted(features, "ha", -1)
    outgoing, meta = route(row_counts, owner_perm, cotangent)
    corner = shifted(from_right, "ha", -1)
    incoming = lax.all_to_all(
        outgoing.reshape(peers, PIX, C), "wa", split_axis=0, concat_axis=0, tiled=True
    )
    from_right, below, corner, incoming = [
        pltpu.with_memory_space_constraint(x, pltpu.VMEM)
        for x in (from_right, below, corner, incoming)
    ]
    pieces = (features, from_right, below, corner)
    places = jnp.concatenate(
        [offsets[:, :SIDE], offsets[:, SIDE:] + (corners[:, 1:2] % 16) * 4], axis=1
    ).astype(F32)
    pad = lambda x: jnp.pad(x, ((0, 0), (0, 2)), constant_values=-1000.0)
    places = jnp.concatenate([pad(places[:, :SIDE]), pad(places[:, SIDE:])], axis=1)
    place_cols = places.T
    corners = corners.T.reshape(-1)
    acts0, acts1, slope0, slope1, turned = forward(
        corners, pieces, place_cols, kernels.reshape(18, C, C)
    )
    inner, keep, send = back(meta, incoming, slope1, slope0, turned, acts1, acts0)
    mine = (keep.astype(F32) + swap_cores(send).astype(F32)).astype(BF)
    parts = lax.all_to_all(mine.reshape(peers, -1, C), "wa", 0, 0, tiled=True)
    tile, right, lower, corner = spread(corners, inner, places, turned)
    corner, lower = [shifted(piece, "ha", 1) for piece in (corner, lower)]
    part = jnp.sum(parts.astype(F32), axis=0).astype(BF)
    count = lax.axis_size("ha")
    total = part.astype(F32)
    for hop in range(2, count, 2):
        moved = lax.ppermute(part, "ha", [(i, (i + hop) % count) for i in range(count)])
        total = total + moved.astype(F32)
    whole = jnp.broadcast_to(total.astype(BF)[None], (peers, *total.shape))
    mine = lax.all_to_all(whole, "wa", 0, 0, tiled=True).reshape(9, C, C)
    side = shifted((right.astype(F32) + corner.astype(F32)).astype(BF), "wa", 1)
    tile = tile + lower.astype(F32)
    mine, tile, side = lax.optimization_barrier((mine, tile, side))
    tile = tile + side.astype(F32)
    other = swap_cores(mine)
    grads = jnp.stack([pick_layer(core, mine, other), pick_layer(core, other, mine)]).astype(F32)
    return (tile, grads.reshape(2, 3, 3, C, C))


def solution(mesh):
    in_specs = (
        P("ha", "wa", None),
        P("ha", "wa"),
        P("ha", None),
        P(("ha", "wa"), None),
        P(("ha", "wa"), None),
        P(),
        P(("ha", "wa"), None, None, None),
    )
    out_specs = (P("ha", "wa", None), P())

    return jax.shard_map(local, mesh=mesh, in_specs=in_specs, out_specs=out_specs, check_vma=False)
```

```python
import jax
import jax.numpy as jnp
from jax import lax
from jax.experimental import pallas as pl
from jax.experimental.pallas import tpu as pltpu
from jax.sharding import PartitionSpec as P

SIDE = 14
PITCH = 16
PIX = SIDE * PITCH
BOX = 32
SPAN = 48
WIN = BOX * SPAN
ROWS = 288
C = 256
BF = jnp.bfloat16
F32 = jnp.float32


def shifted(value, axis, steps):
    count = lax.axis_size(axis)
    first, last = (max(0, -steps), min(count, count - steps))
    return lax.ppermute(value, axis, [(source, source + steps) for source in range(first, last)])


def dot(a, b, dims=(((1,), (0,)), ((), ()))):
    return lax.dot_general(a, b, dims, preferred_element_type=F32)


def inside(rows):
    pixel = lax.broadcasted_iota(jnp.int32, (rows, C), 0)
    return (pixel & (PITCH - 1)) < SIDE


def clear_edges(held, copies):
    for shift in range(3):
        for g in range(copies):
            held[shift, g, 0:16, :] = jnp.zeros((16, C), BF)
            held[shift, g, 16 + PIX : ROWS, :] = jnp.zeros((ROWS - 16 - PIX, C), BF)


def hold(held, g, value):
    held[0, g, 16 : 16 + PIX, :] = pltpu.roll(value, 1, 0).astype(BF)
    held[1, g, 16 : 16 + PIX, :] = value.astype(BF)
    held[2, g, 16 : 16 + PIX, :] = pltpu.roll(value, PIX - 1, 0).astype(BF)


def tent(places, offsets):
    return jnp.maximum(0.0, 1.0 - jnp.abs(places - offsets) * 0.25)


def gelu_parts(v):
    cdf = 0.5 * (1.0 + lax.erf(v * 0.7071067811865476))
    slope = cdf + v * (jnp.exp(v * v * -0.5) * 0.3989422804014327)
    return v * cdf, slope


def route_kernel(count_ref, perm_ref, x_ref, o_ref, meta_ref):
    peers = o_ref.shape[0]
    here = lax.axis_index("wa")
    position = jnp.int32(0)
    for i in range(peers):
        position = jnp.where(perm_ref[0, i] == here, i, position)
    start = jnp.int32(0)
    here_start = jnp.int32(0)
    gap = jnp.zeros((SIDE, PITCH - SIDE, C), BF)
    for i in range(peers):
        here_start = jnp.where(here == i, start, here_start)
        arrival = start + ((position - start) & (peers - 1))
        region = jnp.clip(arrival // peers, 0, x_ref.shape[0] - 1)
        o_ref[i, :, 0:SIDE, :] = x_ref[region]
        o_ref[i, :, SIDE:PITCH, :] = gap
        start = start + count_ref[i, 0, 0]
    for i in range(peers):
        meta_ref[i] = perm_ref[0, (here_start + i) & (peers - 1)]
    meta_ref[peers] = count_ref[here, 0, 0]


def route(counts, perm, cotangent):
    peers = counts.shape[0]
    smem = pl.BlockSpec(memory_space=pltpu.SMEM)
    vmem = pl.BlockSpec(memory_space=pltpu.VMEM)
    return pl.pallas_call(
        route_kernel,
        name="route",
        out_shape=[
            jax.ShapeDtypeStruct((peers, SIDE, PITCH, C), BF),
            jax.ShapeDtypeStruct((peers + 1,), jnp.int32),
        ],
        in_specs=[smem, smem, vmem],
        out_specs=[vmem, smem],
        cost_estimate=pl.CostEstimate(flops=0, bytes_accessed=4 << 20, transcendentals=0),
    )(counts, perm, cotangent)


FG = 4


def forward_kernel(
    corner_ref, tl_ref, tr_ref, bl_ref, br_ref, off_ref, k_ref,
    a0_ref, a1_ref, g0_ref, g1_ref, t_ref, ext, places, row_w, weight, held,
):
    step = pl.program_id(0)

    @pl.when(step == 0)
    def _():
        clear_edges(held, FG)
        ext[0:BOX, 0:BOX, :] = tl_ref[...]
        ext[0:BOX, BOX : 2 * BOX, :] = tr_ref[...]
        ext[BOX : 2 * BOX, 0:BOX, :] = bl_ref[...]
        ext[BOX : 2 * BOX, BOX : 2 * BOX, :] = br_ref[...]
        at = lax.broadcasted_iota(jnp.int32, (16, WIN), 1).astype(F32)
        row = jnp.floor((at + 0.5) * (1.0 / SPAN))
        places[0] = 4.0 * row
        places[1] = 4.0 * (at - SPAN * row)

    keep = inside(PIX)
    lane = lax.broadcasted_iota(jnp.int32, (32, 16), 1)
    for g in range(FG):
        slot = step * FG + g
        top = corner_ref[slot]
        left = pl.multiple_of(corner_ref[16 + slot] // 16 * 16, 16)
        offsets = jnp.sum(jnp.where(lane == slot, off_ref[...], 0.0), axis=1, keepdims=True)
        row_w[g] = tent(places[0], offsets[0:16])
        col_w = tent(places[1], offsets[16:32])
        for i in range(SIDE):
            weight[g, i * PITCH : (i + 1) * PITCH, :] = (row_w[g, i : i + 1, :] * col_w).astype(BF)
        window = ext[pl.ds(top, BOX), pl.ds(left, SPAN), :].reshape(WIN, C)
        hold(held, g, dot(weight[g], window))
        a0_ref[:, g * C : (g + 1) * C] = held[1, g, 16 : 16 + C, :].T
    for i in range(5):
        tap = jnp.minimum(step * 5 + i, 17)
        t_ref[tap] = k_ref[tap].T
    for layer in range(2):
        for g in range(FG):
            pre = jnp.zeros((PIX, C), F32)
            for dy in range(3):
                for dx in range(3):
                    pre += dot(held[dx, g, 16 * dy : 16 * dy + PIX, :], k_ref[layer * 9 + dy * 3 + dx])
            value, slope = gelu_parts(pre)
            slope = jnp.where(keep, slope, 0.0).astype(BF)
            if layer == 0:
                g0_ref[g] = slope
                hold(held, g, jnp.where(keep, value, 0.0))
                a1_ref[:, g * C : (g + 1) * C] = held[1, g, 16 : 16 + C, :].T
            else:
                g1_ref[g] = slope


def forward(corners, pieces, offsets, kernels):
    slots = 16
    whole = lambda *shape: pl.BlockSpec(shape, lambda i, *_: (0,) * len(shape))
    columns = pl.BlockSpec((C, FG * C), lambda i, *_: (0, i))
    regions = pl.BlockSpec((FG, PIX, C), lambda i, *_: (i, 0, 0))
    return pl.pallas_call(
        forward_kernel,
        name="forward",
        out_shape=[
            jax.ShapeDtypeStruct((C, slots * C), BF),
            jax.ShapeDtypeStruct((C, slots * C), BF),
            jax.ShapeDtypeStruct((slots, PIX, C), BF),
            jax.ShapeDtypeStruct((slots, PIX, C), BF),
            jax.ShapeDtypeStruct((18, C, C), BF),
        ],
        grid_spec=pltpu.PrefetchScalarGridSpec(
            num_scalar_prefetch=1,
            grid=(slots // FG,),
            in_specs=[
                whole(BOX, BOX, C),
                pl.BlockSpec(memory_space=pltpu.VMEM),
                pl.BlockSpec(memory_space=pltpu.VMEM),
                pl.BlockSpec(memory_space=pltpu.VMEM),
                whole(32, 16),
                whole(18, C, C),
            ],
            out_specs=[columns, columns, regions, regions, whole(18, C, C)],
            scratch_shapes=[
                pltpu.VMEM((2 * BOX, 2 * BOX, C), BF),
                pltpu.VMEM((2, 16, WIN), F32),
                pltpu.VMEM((FG, 16, WIN), F32),
                pltpu.VMEM((FG, PIX, WIN), BF),
                pltpu.VMEM((3, FG, ROWS, C), BF),
            ],
        ),
        cost_estimate=pl.CostEstimate(
            flops=11_300_000_000, bytes_accessed=14 << 20, transcendentals=4_000_000
        ),
    )(corners, *pieces, offsets, kernels)


BG = 4


def top_grad(meta_ref, slot, in_ref, slope):
    live = slot < meta_ref[16]
    grad = in_ref[meta_ref[jnp.minimum(slot, 15)]].astype(F32) * slope.astype(F32)
    return jnp.where(live, grad, 0.0)


def add_tap(held, a_ref, acc, tap):
    dy, dx = divmod(tap, 3)
    grads = held[2 - dx, :, 32 - 16 * dy : 32 - 16 * dy + C, :].reshape(BG * C, C)
    acc[tap] += dot(a_ref[...], grads)


def input_grad(held, g, k_ref):
    total = jnp.zeros((PIX, C), F32)
    for dy in range(3):
        for dx in range(3):
            total += dot(
                held[2 - dx, g, 32 - 16 * dy : 32 - 16 * dy + PIX, :],
                k_ref[dy * 3 + dx],
            )
    return total.astype(BF)


def back_kernel(
    meta_ref, in_ref, first_ref, next_ref, g0_ref, k_ref, a1_ref, a0_ref,
    p_ref, keep_ref, send_ref, upper, held, acc1, acc0,
):
    step = pl.program_id(0)
    now = step & 1

    @pl.when(step == 0)
    def _():
        clear_edges(upper.at[0], BG)
        clear_edges(upper.at[1], BG)
        clear_edges(held, BG)
        acc1[...] = jnp.zeros_like(acc1)
        acc0[...] = jnp.zeros_like(acc0)
        for g in range(BG):
            hold(upper.at[0], g, top_grad(meta_ref, g, in_ref, first_ref[g]))

    here = upper.at[now]
    later = upper.at[1 - now]

    def inner_grad(g, grad):
        grad = grad.astype(F32) * g0_ref[g].astype(F32)
        p_ref[g] = grad.astype(BF)
        hold(held, g, grad)

    grads = [input_grad(here, 0, k_ref)]
    for g in range(1, BG):
        grads.append(input_grad(here, g, k_ref))
        inner_grad(g - 1, grads[g - 1])
    for tap in range(9):
        add_tap(here, a1_ref, acc1, tap)
        if tap == 0:
            inner_grad(BG - 1, grads[BG - 1])
    for tap in range(9):
        add_tap(held, a0_ref, acc0, tap)
        if tap % 2 == 0 and tap // 2 < BG:
            g = tap // 2
            hold(later, g, top_grad(meta_ref, (step + 1) * BG + g, in_ref, next_ref[g]))

    @pl.when(step == pl.num_programs(0) - 1)
    def _():
        keeps_first = (lax.axis_index("ha") & 1) == 0

        @pl.when(keeps_first)
        def _():
            keep_ref[...] = acc0[...].astype(BF)
            send_ref[...] = acc1[...].astype(BF)

        @pl.when(jnp.logical_not(keeps_first))
        def _():
            keep_ref[...] = acc1[...].astype(BF)
            send_ref[...] = acc0[...].astype(BF)


def back(meta, incoming, slope1, slope0, kernels, acts1, acts0):
    slots = slope1.shape[0]
    steps = slots // BG
    whole = lambda *shape: pl.BlockSpec(shape, lambda i, *_: (0,) * len(shape))
    regions = pl.BlockSpec((BG, PIX, C), lambda i, *_: (i, 0, 0))
    columns = pl.BlockSpec((C, BG * C), lambda i, *_: (0, i))
    return pl.pallas_call(
        back_kernel,
        name="back",
        out_shape=[
            jax.ShapeDtypeStruct((slots, PIX, C), BF),
            pltpu.VMEM((9, C, C), BF),
            pltpu.VMEM((9, C, C), BF),
        ],
        grid_spec=pltpu.PrefetchScalarGridSpec(
            num_scalar_prefetch=1,
            grid=(steps,),
            in_specs=[
                pl.BlockSpec(memory_space=pltpu.VMEM),
                whole(BG, PIX, C),
                pl.BlockSpec((BG, PIX, C), lambda i, *_: (jnp.minimum(i + 1, steps - 1), 0, 0)),
                regions,
                pl.BlockSpec((9, C, C), lambda i, *_: (1, 0, 0)),
                columns,
                columns,
            ],
            out_specs=[regions] + [pl.BlockSpec(memory_space=pltpu.VMEM)] * 2,
            scratch_shapes=[
                pltpu.VMEM((2, 3, BG, ROWS, C), BF),
                pltpu.VMEM((3, BG, ROWS, C), BF),
                pltpu.VMEM((9, C, C), F32),
                pltpu.VMEM((9, C, C), F32),
            ],
        ),
        compiler_params=pltpu.CompilerParams(vmem_limit_bytes=58 << 20),
        cost_estimate=pl.CostEstimate(
            flops=14_000_000_000, bytes_accessed=16 << 20, transcendentals=0
        ),
    )(meta, incoming, slope1, slope1, slope0, kernels, acts1, acts0)


SG = 4
PART = 4


def spread_kernel(
    corner_ref, p_ref, off_ref, k_ref, tl_ref, tr_ref, bl_ref, br_ref, held, row_w, lanes, total
):
    step = pl.program_id(0)

    @pl.when(step == 0)
    def _():
        clear_edges(held, SG)
        total[...] = jnp.zeros_like(total)
        entry = lax.broadcasted_iota(jnp.int32, (32, C), 0)
        pixel = lax.broadcasted_iota(jnp.int32, (32, C), 1)
        for axis in range(2):
            index = pixel // PITCH if axis == 0 else 16 + (pixel & (PITCH - 1))
            pick = jnp.where(entry == index, 1.0, 0.0).astype(BF)
            lanes[axis] = dot(off_ref[...].astype(BF), pick)

    for g in range(SG):
        hold(held, g, p_ref[g].astype(F32))
    row_at = 4.0 * lax.broadcasted_iota(jnp.int32, (BOX, C), 0).astype(F32)
    col_at = 4.0 * lax.broadcasted_iota(jnp.int32, (SPAN, C), 0).astype(F32)
    grads = [
        jnp.concatenate([input_grad(held, g, k_ref), jnp.zeros((C - PIX, C), BF)], axis=0)
        for g in range(SG)
    ]
    for g in range(SG):
        slot = step * SG + g
        top = corner_ref[slot]
        left = pl.multiple_of(corner_ref[16 + slot] // 16 * 16, 16)
        row_w[g] = tent(row_at, lanes[0, pl.ds(slot, 1), :])
        col_w = tent(col_at, lanes[1, pl.ds(slot, 1), :])
        for at in range(0, BOX, PART):
            weight = jnp.concatenate(
                [(row_w[g, p : p + 1, :] * col_w).astype(BF) for p in range(at, at + PART)], axis=0
            )
            total[pl.ds(top + at, PART), pl.ds(left, SPAN), :] += dot(weight, grads[g]).reshape(
                PART, SPAN, C
            )

    @pl.when(step == pl.num_programs(0) - 1)
    def _():
        tl_ref[...] = total[0:BOX, 0:BOX, :]
        tr_ref[...] = total[0:BOX, BOX : 2 * BOX, :].astype(BF)
        bl_ref[...] = total[BOX : 2 * BOX, 0:BOX, :].astype(BF)
        br_ref[...] = total[BOX : 2 * BOX, BOX : 2 * BOX, :].astype(BF)


def spread(corners, inner, offsets, kernels):
    slots = inner.shape[0]
    whole = lambda *shape: pl.BlockSpec(shape, lambda i, *_: (0,) * len(shape))
    piece = lambda kind: jax.ShapeDtypeStruct((BOX, BOX, C), kind)
    return pl.pallas_call(
        spread_kernel,
        name="spread",
        out_shape=[piece(F32), piece(BF), piece(BF), piece(BF)],
        grid_spec=pltpu.PrefetchScalarGridSpec(
            num_scalar_prefetch=1,
            grid=(slots // SG,),
            in_specs=[
                pl.BlockSpec((SG, PIX, C), lambda i, *_: (i, 0, 0)),
                whole(16, 32),
                whole(9, C, C),
            ],
            out_specs=[whole(BOX, BOX, C)] * 4,
            scratch_shapes=[
                pltpu.VMEM((3, SG, ROWS, C), BF),
                pltpu.VMEM((SG, BOX, C), F32),
                pltpu.VMEM((2, 16, C), F32),
                pltpu.VMEM((2 * BOX, 2 * BOX, C), F32),
            ],
        ),
        cost_estimate=pl.CostEstimate(
            flops=7_000_000_000, bytes_accessed=6 << 20, transcendentals=0
        ),
    )(corners, inner, offsets, kernels)


def swap_cores(x):
    return lax.ppermute(x, "ha", [(i, i ^ 1) for i in range(lax.axis_size("ha"))])


def pick_layer(index, first, second):
    return jnp.where(index == 0, first, second)


def local(features, counts, owner_perm, corners, offsets, kernels, cotangent):
    peers = lax.axis_size("wa")
    core = lax.axis_index("ha") % 2
    row_counts = lax.all_to_all(
        jnp.broadcast_to(counts[None], (peers, 1, 1)), "wa", 0, 0, tiled=True
    )
    from_right = shifted(features, "wa", -1)
    below = shifted(features, "ha", -1)
    outgoing, meta = route(row_counts, owner_perm, cotangent)
    corner = shifted(from_right, "ha", -1)
    incoming = lax.all_to_all(
        outgoing.reshape(peers, PIX, C), "wa", split_axis=0, concat_axis=0, tiled=True
    )
    from_right, below, corner, incoming = [
        pltpu.with_memory_space_constraint(x, pltpu.VMEM)
        for x in (from_right, below, corner, incoming)
    ]
    pieces = (features, from_right, below, corner)
    places = jnp.concatenate(
        [offsets[:, :SIDE], offsets[:, SIDE:] + (corners[:, 1:2] % 16) * 4], axis=1
    ).astype(F32)
    pad = lambda x: jnp.pad(x, ((0, 0), (0, 2)), constant_values=-1000.0)
    places = jnp.concatenate([pad(places[:, :SIDE]), pad(places[:, SIDE:])], axis=1)
    place_cols = places.T
    corners = corners.T.reshape(-1)
    acts0, acts1, slope0, slope1, turned = forward(
        corners, pieces, place_cols, kernels.reshape(18, C, C)
    )
    inner, keep, send = back(meta, incoming, slope1, slope0, turned, acts1, acts0)
    mine = (keep.astype(F32) + swap_cores(send).astype(F32)).astype(BF)
    parts = lax.all_to_all(mine.reshape(peers, -1, C), "wa", 0, 0, tiled=True)
    tile, right, lower, corner = spread(corners, inner, places, turned)
    corner = shifted(corner, "ha", 1)
    lower = shifted(lower, "ha", 1)
    part = jnp.sum(parts.astype(F32), axis=0).astype(BF)
    count = lax.axis_size("ha")
    total = part.astype(F32)
    for hop in range(2, count, 2):
        moved = lax.ppermute(part, "ha", [(i, (i + hop) % count) for i in range(count)])
        total = total + moved.astype(F32)
    whole = jnp.broadcast_to(total.astype(BF)[None], (peers, *total.shape))
    mine = lax.all_to_all(whole, "wa", 0, 0, tiled=True).reshape(9, C, C)
    side = shifted((right.astype(F32) + corner.astype(F32)).astype(BF), "wa", 1)
    tile = tile + lower.astype(F32) + side.astype(F32)
    mine, tile = lax.optimization_barrier((mine, tile))
    other = swap_cores(mine)
    grads = jnp.stack([pick_layer(core, mine, other), pick_layer(core, other, mine)]).astype(F32)
    return (tile, grads.reshape(2, 3, 3, C, C))


def solution(mesh):
    in_specs = (
        P("ha", "wa", None),
        P("ha", "wa"),
        P("ha", None),
        P(("ha", "wa"), None),
        P(("ha", "wa"), None),
        P(),
        P(("ha", "wa"), None, None, None),
    )
    out_specs = (P("ha", "wa", None), P())

    return jax.shard_map(local, mesh=mesh, in_specs=in_specs, out_specs=out_specs, check_vma=False)
```

```python
import jax
import jax.numpy as jnp
from jax import lax
from jax.experimental import pallas as pl
from jax.experimental.pallas import tpu as pltpu
from jax.sharding import PartitionSpec as P

SIDE = 14
PITCH = 16
PIX = SIDE * PITCH
BOX = 32
SPAN = 48
WIN = BOX * SPAN
ROWS = 288
C = 256
BF = jnp.bfloat16
F32 = jnp.float32


def shifted(value, axis, steps):
    count = lax.axis_size(axis)
    first, last = (max(0, -steps), min(count, count - steps))
    return lax.ppermute(value, axis, [(source, source + steps) for source in range(first, last)])


def dot(a, b, dims=(((1,), (0,)), ((), ()))):
    return lax.dot_general(a, b, dims, preferred_element_type=F32)


def inside(rows):
    pixel = lax.broadcasted_iota(jnp.int32, (rows, C), 0)
    return (pixel & (PITCH - 1)) < SIDE


def clear_edges(held, copies):
    for shift in range(3):
        for g in range(copies):
            held[shift, g, 0:16, :] = jnp.zeros((16, C), BF)
            held[shift, g, 16 + PIX : ROWS, :] = jnp.zeros((ROWS - 16 - PIX, C), BF)


def hold(held, g, value):
    held[0, g, 16 : 16 + PIX, :] = pltpu.roll(value, 1, 0).astype(BF)
    held[1, g, 16 : 16 + PIX, :] = value.astype(BF)
    held[2, g, 16 : 16 + PIX, :] = pltpu.roll(value, PIX - 1, 0).astype(BF)


def tent(places, offsets):
    return jnp.maximum(0.0, 1.0 - jnp.abs(places - offsets) * 0.25)


def gelu_parts(v):
    cdf = 0.5 * (1.0 + lax.erf(v * 0.7071067811865476))
    slope = cdf + v * (jnp.exp(v * v * -0.5) * 0.3989422804014327)
    return v * cdf, slope


def route_kernel(count_ref, perm_ref, x_ref, o_ref, meta_ref):
    peers = o_ref.shape[0]
    here = lax.axis_index("wa")
    position = jnp.int32(0)
    for i in range(peers):
        position = jnp.where(perm_ref[0, i] == here, i, position)
    start = jnp.int32(0)
    here_start = jnp.int32(0)
    gap = jnp.zeros((SIDE, PITCH - SIDE, C), BF)
    for i in range(peers):
        here_start = jnp.where(here == i, start, here_start)
        arrival = start + ((position - start) & (peers - 1))
        region = jnp.clip(arrival // peers, 0, x_ref.shape[0] - 1)
        o_ref[i, :, 0:SIDE, :] = x_ref[region]
        o_ref[i, :, SIDE:PITCH, :] = gap
        start = start + count_ref[i, 0, 0]
    for i in range(peers):
        meta_ref[i] = perm_ref[0, (here_start + i) & (peers - 1)]
    meta_ref[peers] = count_ref[here, 0, 0]


def route(counts, perm, cotangent):
    peers = counts.shape[0]
    smem = pl.BlockSpec(memory_space=pltpu.SMEM)
    vmem = pl.BlockSpec(memory_space=pltpu.VMEM)
    return pl.pallas_call(
        route_kernel,
        name="route",
        out_shape=[
            jax.ShapeDtypeStruct((peers, SIDE, PITCH, C), BF),
            jax.ShapeDtypeStruct((peers + 1,), jnp.int32),
        ],
        in_specs=[smem, smem, vmem],
        out_specs=[vmem, smem],
        cost_estimate=pl.CostEstimate(flops=0, bytes_accessed=4 << 20, transcendentals=0),
    )(counts, perm, cotangent)


FG = 4


def forward_kernel(
    corner_ref, tl_ref, tr_ref, bl_ref, br_ref, off_ref, k_ref,
    a0_ref, a1_ref, g0_ref, g1_ref, t_ref, ext, places, row_w, weight, held,
):
    step = pl.program_id(0)

    @pl.when(step == 0)
    def _():
        clear_edges(held, FG)
        ext[0:BOX, 0:BOX, :] = tl_ref[...]
        ext[0:BOX, BOX : 2 * BOX, :] = tr_ref[...]
        ext[BOX : 2 * BOX, 0:BOX, :] = bl_ref[...]
        ext[BOX : 2 * BOX, BOX : 2 * BOX, :] = br_ref[...]
        at = lax.broadcasted_iota(jnp.int32, (16, WIN), 1).astype(F32)
        row = jnp.floor((at + 0.5) * (1.0 / SPAN))
        places[0] = 4.0 * row
        places[1] = 4.0 * (at - SPAN * row)

    keep = inside(PIX)
    lane = lax.broadcasted_iota(jnp.int32, (32, 16), 1)
    for g in range(FG):
        slot = step * FG + g
        top = corner_ref[slot]
        left = pl.multiple_of(corner_ref[16 + slot] // 16 * 16, 16)
        offsets = jnp.sum(jnp.where(lane == slot, off_ref[...], 0.0), axis=1, keepdims=True)
        row_w[g] = tent(places[0], offsets[0:16])
        col_w = tent(places[1], offsets[16:32])
        for i in range(SIDE):
            weight[g, i * PITCH : (i + 1) * PITCH, :] = (row_w[g, i : i + 1, :] * col_w).astype(BF)
        window = ext[pl.ds(top, BOX), pl.ds(left, SPAN), :].reshape(WIN, C)
        hold(held, g, dot(weight[g], window))
        a0_ref[:, g * C : (g + 1) * C] = held[1, g, 16 : 16 + C, :].T
    for i in range(5):
        tap = jnp.minimum(step * 5 + i, 17)
        t_ref[tap] = k_ref[tap].T
    for layer in range(2):
        for g in range(FG):
            pre = jnp.zeros((PIX, C), F32)
            for dy in range(3):
                for dx in range(3):
                    pre += dot(held[dx, g, 16 * dy : 16 * dy + PIX, :], k_ref[layer * 9 + dy * 3 + dx])
            value, slope = gelu_parts(pre)
            slope = jnp.where(keep, slope, 0.0).astype(BF)
            if layer == 0:
                g0_ref[g] = slope
                hold(held, g, jnp.where(keep, value, 0.0))
                a1_ref[:, g * C : (g + 1) * C] = held[1, g, 16 : 16 + C, :].T
            else:
                g1_ref[g] = slope


def forward(corners, pieces, offsets, kernels):
    slots = 16
    whole = lambda *shape: pl.BlockSpec(shape, lambda i, *_: (0,) * len(shape))
    columns = pl.BlockSpec((C, FG * C), lambda i, *_: (0, i))
    regions = pl.BlockSpec((FG, PIX, C), lambda i, *_: (i, 0, 0))
    return pl.pallas_call(
        forward_kernel,
        name="forward",
        out_shape=[
            jax.ShapeDtypeStruct((C, slots * C), BF),
            jax.ShapeDtypeStruct((C, slots * C), BF),
            jax.ShapeDtypeStruct((slots, PIX, C), BF),
            jax.ShapeDtypeStruct((slots, PIX, C), BF),
            jax.ShapeDtypeStruct((18, C, C), BF),
        ],
        grid_spec=pltpu.PrefetchScalarGridSpec(
            num_scalar_prefetch=1,
            grid=(slots // FG,),
            in_specs=[
                whole(BOX, BOX, C),
                pl.BlockSpec(memory_space=pltpu.VMEM),
                pl.BlockSpec(memory_space=pltpu.VMEM),
                pl.BlockSpec(memory_space=pltpu.VMEM),
                whole(32, 16),
                whole(18, C, C),
            ],
            out_specs=[columns, columns, regions, regions, whole(18, C, C)],
            scratch_shapes=[
                pltpu.VMEM((2 * BOX, 2 * BOX, C), BF),
                pltpu.VMEM((2, 16, WIN), F32),
                pltpu.VMEM((FG, 16, WIN), F32),
                pltpu.VMEM((FG, PIX, WIN), BF),
                pltpu.VMEM((3, FG, ROWS, C), BF),
            ],
        ),
        cost_estimate=pl.CostEstimate(
            flops=11_300_000_000, bytes_accessed=14 << 20, transcendentals=4_000_000
        ),
    )(corners, *pieces, offsets, kernels)


BG = 4


def top_grad(meta_ref, slot, in_ref, slope):
    live = slot < meta_ref[16]
    grad = in_ref[meta_ref[jnp.minimum(slot, 15)]].astype(F32) * slope.astype(F32)
    return jnp.where(live, grad, 0.0)


def add_tap(held, a_ref, acc, tap):
    dy, dx = divmod(tap, 3)
    grads = held[2 - dx, :, 32 - 16 * dy : 32 - 16 * dy + C, :].reshape(BG * C, C)
    acc[tap] += dot(a_ref[...], grads)


def input_grad(held, g, k_ref):
    total = jnp.zeros((PIX, C), F32)
    for dy in range(3):
        for dx in range(3):
            total += dot(
                held[2 - dx, g, 32 - 16 * dy : 32 - 16 * dy + PIX, :],
                k_ref[dy * 3 + dx],
            )
    return total.astype(BF)


def back_kernel(
    meta_ref, in_ref, first_ref, next_ref, g0_ref, k_ref, a1_ref, a0_ref,
    p_ref, keep_ref, send_ref, upper, held, acc1, acc0,
):
    step = pl.program_id(0)
    now = step & 1

    @pl.when(step == 0)
    def _():
        clear_edges(upper.at[0], BG)
        clear_edges(upper.at[1], BG)
        clear_edges(held, BG)
        acc1[...] = jnp.zeros_like(acc1)
        acc0[...] = jnp.zeros_like(acc0)
        for g in range(BG):
            hold(upper.at[0], g, top_grad(meta_ref, g, in_ref, first_ref[g]))

    here = upper.at[now]
    later = upper.at[1 - now]

    def inner_grad(g, grad):
        grad = grad.astype(F32) * g0_ref[g].astype(F32)
        p_ref[g] = grad.astype(BF)
        hold(held, g, grad)

    grads = [input_grad(here, 0, k_ref)]
    for g in range(1, BG):
        grads.append(input_grad(here, g, k_ref))
        inner_grad(g - 1, grads[g - 1])
    for tap in range(9):
        add_tap(here, a1_ref, acc1, tap)
        if tap == 0:
            inner_grad(BG - 1, grads[BG - 1])
    for tap in range(9):
        add_tap(held, a0_ref, acc0, tap)
        if tap % 2 == 0 and tap // 2 < BG:
            g = tap // 2
            hold(later, g, top_grad(meta_ref, (step + 1) * BG + g, in_ref, next_ref[g]))

    @pl.when(step == pl.num_programs(0) - 1)
    def _():
        keeps_first = (lax.axis_index("ha") & 1) == 0

        @pl.when(keeps_first)
        def _():
            keep_ref[...] = acc0[...].astype(BF)
            send_ref[...] = acc1[...].astype(BF)

        @pl.when(jnp.logical_not(keeps_first))
        def _():
            keep_ref[...] = acc1[...].astype(BF)
            send_ref[...] = acc0[...].astype(BF)


def back(meta, incoming, slope1, slope0, kernels, acts1, acts0):
    slots = slope1.shape[0]
    steps = slots // BG
    whole = lambda *shape: pl.BlockSpec(shape, lambda i, *_: (0,) * len(shape))
    regions = pl.BlockSpec((BG, PIX, C), lambda i, *_: (i, 0, 0))
    columns = pl.BlockSpec((C, BG * C), lambda i, *_: (0, i))
    return pl.pallas_call(
        back_kernel,
        name="back",
        out_shape=[
            jax.ShapeDtypeStruct((slots, PIX, C), BF),
            pltpu.VMEM((9, C, C), BF),
            pltpu.VMEM((9, C, C), BF),
        ],
        grid_spec=pltpu.PrefetchScalarGridSpec(
            num_scalar_prefetch=1,
            grid=(steps,),
            in_specs=[
                pl.BlockSpec(memory_space=pltpu.VMEM),
                whole(BG, PIX, C),
                pl.BlockSpec((BG, PIX, C), lambda i, *_: (jnp.minimum(i + 1, steps - 1), 0, 0)),
                regions,
                pl.BlockSpec((9, C, C), lambda i, *_: (1, 0, 0)),
                columns,
                columns,
            ],
            out_specs=[regions] + [pl.BlockSpec(memory_space=pltpu.VMEM)] * 2,
            scratch_shapes=[
                pltpu.VMEM((2, 3, BG, ROWS, C), BF),
                pltpu.VMEM((3, BG, ROWS, C), BF),
                pltpu.VMEM((9, C, C), F32),
                pltpu.VMEM((9, C, C), F32),
            ],
        ),
        compiler_params=pltpu.CompilerParams(vmem_limit_bytes=58 << 20),
        cost_estimate=pl.CostEstimate(
            flops=14_000_000_000, bytes_accessed=16 << 20, transcendentals=0
        ),
    )(meta, incoming, slope1, slope1, slope0, kernels, acts1, acts0)


SG = 4
PART = 4


def spread_kernel(
    corner_ref, p_ref, off_ref, k_ref, tl_ref, tr_ref, bl_ref, br_ref, held, row_w, lanes, total
):
    step = pl.program_id(0)

    @pl.when(step == 0)
    def _():
        clear_edges(held, SG)
        total[...] = jnp.zeros_like(total)
        entry = lax.broadcasted_iota(jnp.int32, (32, C), 0)
        pixel = lax.broadcasted_iota(jnp.int32, (32, C), 1)
        for axis in range(2):
            index = pixel // PITCH if axis == 0 else 16 + (pixel & (PITCH - 1))
            pick = jnp.where(entry == index, 1.0, 0.0).astype(BF)
            lanes[axis] = dot(off_ref[...].astype(BF), pick)

    for g in range(SG):
        hold(held, g, p_ref[g].astype(F32))
    row_at = 4.0 * lax.broadcasted_iota(jnp.int32, (BOX, C), 0).astype(F32)
    col_at = 4.0 * lax.broadcasted_iota(jnp.int32, (SPAN, C), 0).astype(F32)
    grads = [
        jnp.concatenate([input_grad(held, g, k_ref), jnp.zeros((C - PIX, C), BF)], axis=0)
        for g in range(SG)
    ]
    for g in range(SG):
        slot = step * SG + g
        top = corner_ref[slot]
        left = pl.multiple_of(corner_ref[16 + slot] // 16 * 16, 16)
        row_w[g] = tent(row_at, lanes[0, pl.ds(slot, 1), :])
        col_w = tent(col_at, lanes[1, pl.ds(slot, 1), :])
        for at in range(0, BOX, PART):
            weight = jnp.concatenate(
                [(row_w[g, p : p + 1, :] * col_w).astype(BF) for p in range(at, at + PART)], axis=0
            )
            total[pl.ds(top + at, PART), pl.ds(left, SPAN), :] += dot(weight, grads[g]).reshape(
                PART, SPAN, C
            )

    @pl.when(step == pl.num_programs(0) - 1)
    def _():
        tl_ref[...] = total[0:BOX, 0:BOX, :]
        tr_ref[...] = total[0:BOX, BOX : 2 * BOX, :].astype(BF)
        bl_ref[...] = total[BOX : 2 * BOX, 0:BOX, :].astype(BF)
        br_ref[...] = total[BOX : 2 * BOX, BOX : 2 * BOX, :].astype(BF)


def spread(corners, inner, offsets, kernels):
    slots = inner.shape[0]
    whole = lambda *shape: pl.BlockSpec(shape, lambda i, *_: (0,) * len(shape))
    piece = lambda kind: jax.ShapeDtypeStruct((BOX, BOX, C), kind)
    return pl.pallas_call(
        spread_kernel,
        name="spread",
        out_shape=[piece(F32), piece(BF), piece(BF), piece(BF)],
        grid_spec=pltpu.PrefetchScalarGridSpec(
            num_scalar_prefetch=1,
            grid=(slots // SG,),
            in_specs=[
                pl.BlockSpec((SG, PIX, C), lambda i, *_: (i, 0, 0)),
                whole(16, 32),
                whole(9, C, C),
            ],
            out_specs=[whole(BOX, BOX, C)] * 4,
            scratch_shapes=[
                pltpu.VMEM((3, SG, ROWS, C), BF),
                pltpu.VMEM((SG, BOX, C), F32),
                pltpu.VMEM((2, 16, C), F32),
                pltpu.VMEM((2 * BOX, 2 * BOX, C), F32),
            ],
        ),
        cost_estimate=pl.CostEstimate(
            flops=7_000_000_000, bytes_accessed=6 << 20, transcendentals=0
        ),
    )(corners, inner, offsets, kernels)


def swap_cores(x):
    return lax.ppermute(x, "ha", [(i, i ^ 1) for i in range(lax.axis_size("ha"))])


def local(features, counts, owner_perm, corners, offsets, kernels, cotangent):
    peers = lax.axis_size("wa")
    core = lax.axis_index("ha") % 2
    row_counts = lax.all_to_all(
        jnp.broadcast_to(counts[None], (peers, 1, 1)), "wa", 0, 0, tiled=True
    )
    from_right = shifted(features, "wa", -1)
    below = shifted(features, "ha", -1)
    outgoing, meta = route(row_counts, owner_perm, cotangent)
    corner = shifted(from_right, "ha", -1)
    incoming = lax.all_to_all(
        outgoing.reshape(peers, PIX, C), "wa", split_axis=0, concat_axis=0, tiled=True
    )
    from_right, below, corner, incoming = [
        pltpu.with_memory_space_constraint(x, pltpu.VMEM)
        for x in (from_right, below, corner, incoming)
    ]
    pieces = (features, from_right, below, corner)
    places = jnp.concatenate(
        [offsets[:, :SIDE], offsets[:, SIDE:] + (corners[:, 1:2] % 16) * 4], axis=1
    ).astype(F32)
    pad = lambda x: jnp.pad(x, ((0, 0), (0, 2)), constant_values=-1000.0)
    places = jnp.concatenate([pad(places[:, :SIDE]), pad(places[:, SIDE:])], axis=1)
    place_cols = places.T
    corners = corners.T.reshape(-1)
    acts0, acts1, slope0, slope1, turned = forward(
        corners, pieces, place_cols, kernels.reshape(18, C, C)
    )
    inner, keep, send = back(meta, incoming, slope1, slope0, turned, acts1, acts0)
    mine = (keep.astype(F32) + swap_cores(send).astype(F32)).astype(BF)
    parts = lax.all_to_all(mine.reshape(peers, -1, C), "wa", 0, 0, tiled=True)
    tile, right, lower, corner = spread(corners, inner, places, turned)
    corner = shifted(corner, "ha", 1)
    lower = shifted(lower, "ha", 1)
    part = jnp.sum(parts.astype(F32), axis=0).astype(BF)
    count = lax.axis_size("ha")
    total = part.astype(F32)
    for hop in range(2, count, 2):
        moved = lax.ppermute(part, "ha", [(i, (i + hop) % count) for i in range(count)])
        total = total + moved.astype(F32)
    whole = jnp.broadcast_to(total.astype(BF)[None], (peers, *total.shape))
    mine = lax.all_to_all(whole, "wa", 0, 0, tiled=True).reshape(9, C, C)
    side = shifted((right.astype(F32) + corner.astype(F32)).astype(BF), "wa", 1)
    tile = tile + lower.astype(F32) + side.astype(F32)
    mine, tile = lax.optimization_barrier((mine, tile))
    grads = jnp.zeros((2, *mine.shape), F32)
    grads = lax.dynamic_update_slice(grads, mine.astype(F32)[None], (core, 0, 0, 0))
    other = swap_cores(mine)
    grads = lax.dynamic_update_slice(grads, other.astype(F32)[None], (1 - core, 0, 0, 0))
    return (tile, grads.reshape(2, 3, 3, C, C))


def solution(mesh):
    in_specs = (
        P("ha", "wa", None),
        P("ha", "wa"),
        P("ha", None),
        P(("ha", "wa"), None),
        P(("ha", "wa"), None),
        P(),
        P(("ha", "wa"), None, None, None),
    )
    out_specs = (P("ha", "wa", None), P())

    return jax.shard_map(local, mesh=mesh, in_specs=in_specs, out_specs=out_specs, check_vma=False)
```
